32 devices in a mesh: ctx: 16 (over z, y, core), wt: 2 (over x).
Axes of the slice: x: 2, y: 2, z: 4, core: 2. Of those that a mesh axis runs over, the one named last changes fastest.
Arguments:
- block_input: bfloat16 [2, 2048, 896], P('wt', 'ctx'), may hold values from -40 to 40
- cotangent: bfloat16 [2, 2048, 896], P('wt', 'ctx'), may hold values from -6 to 6
- norm_attn: float32 [896], replicated, may hold values from 0.1 to 1.9
- w_qkv: bfloat16 [896, 1152], P('wt'), may hold values from -1 to 1
- b_qkv: float32 [1152], replicated, may hold values from -3 to 3
- w_out: bfloat16 [896, 896], P('wt'), may hold values from -3 to 3
- norm_mlp: float32 [896], replicated, may hold values from 0.1 to 1.9
- w_gate: bfloat16 [896, 4864], P('wt'), may hold values from -0.1875 to 0.1875
- w_up: bfloat16 [896, 4864], P('wt'), may hold values from -0.1875 to 0.1875
- w_down: bfloat16 [4864, 896], P('wt'), may hold values from -0.078125 to 0.078125
Outputs:
- block_output: bfloat16 [2, 2048, 896], P('wt', 'ctx')
- grad_input: float32 [2, 2048, 896], P('wt', 'ctx')
- grad_norm_attn: float32 [896], P(('ctx', 'wt'))
- grad_w_qkv: float32 [896, 1152], P(('ctx', 'wt'))
- grad_b_qk: float32 [1024], P(('ctx', 'wt'))
- grad_b_v: float32 [128], P(('ctx', 'wt'))
- grad_w_out: float32 [896, 896], P(('ctx', 'wt'))
- grad_norm_mlp: float32 [896], P(('ctx', 'wt'))
- grad_w_gate: float32 [896, 4864], P(('ctx', 'wt'))
- grad_w_up: float32 [896, 4864], P(('ctx', 'wt'))
- grad_w_down: float32 [4864, 896], P(('ctx', 'wt'))
The draws below stay inside these ranges and needn't reach their ends.
All inputs are finite; a program needn't handle non-finite values.
Results may differ from the reference program's by a relative error of at most 0.035.
Values may be sent and summed in bfloat16 or wider, within the bound.
No kernel may reach another device: no remote copies, remote signals or barrier semaphores. Data moves between devices by JAX's collectives and lax.ppermute only.
A program may use at most 320 MiB of HBM per device.

```python
import math
import jax
import jax.numpy as jnp
from jax import lax

D = 896
H = 14
KVH = 2
HD = 64
FF = 4864
TOK_DEV = 128
QKV = 1152
LENGTH = 2048
SEQS = 2


def draw_block_input(key, part):
    key_base, key_cols, key_rows = jax.random.split(key, 3)
    full_shape = (SEQS, LENGTH, D)
    columns = jnp.exp(jax.random.uniform(key_cols, (D,), jnp.float32, math.log(0.3), math.log(3.0)))
    row_scale = jnp.exp(jax.random.uniform(key_rows, (SEQS, LENGTH, 1), jnp.float32, math.log(0.3), math.log(3.0)))
    base_draw = jnp.clip(jax.random.normal(key_base, full_shape, jnp.float32), -4.0, 4.0)
    return (base_draw * columns * row_scale).astype(jnp.bfloat16)


def draw_w_qkv(key, part):
    scale_w = D ** (-0.5)
    return (jnp.clip(jax.random.normal(key, (D, QKV), jnp.float32), -5.0, 5.0) * scale_w).astype(jnp.bfloat16)


def steps_of(rng, shape, cuts, low, top_value):
    level = 1.0
    for dim, blocks in cuts:
        heights = jax.random.uniform(jax.random.fold_in(jax.random.fold_in(rng, 6), dim), (blocks,), jnp.float32, low / len(cuts), top_value / len(cuts))
        level = level * jnp.repeat(jnp.exp(heights), shape[dim] // blocks).reshape((-1,) + (1,) * (len(shape) - 1 - dim))
    return level


def bell_draw(key, extent, scale, bound, cuts=(), kind=jnp.bfloat16):
    array = jax.random.normal(key, extent, jnp.float32) * scale
    if len(cuts) > 0:
        array = steps_of(key, extent, cuts, -0.22, 0.18) * array
    return jnp.clip(array, min=-bound, max=bound).astype(kind)


def setup_inputs(seed: int = 0) -> dict:
    streams_of = jax.random.split(jax.random.key(seed), 11)
    block_input = draw_block_input(jax.random.fold_in(streams_of[10], 71), 0)
    cotangent = bell_draw(streams_of[1], (SEQS, LENGTH, D), 1.0, 6.0, ((0, 2), (1, 16)))
    norm_attn = jnp.clip(1.0 + 0.18 * jax.random.normal(streams_of[2], (D,), jnp.float32), 0.1, 1.9)
    w_qkv = draw_w_qkv(jax.random.fold_in(streams_of[10], 71), 0)
    b_qkv = bell_draw(streams_of[4], (QKV,), 0.5, 3.0, (), jnp.float32)
    w_out = bell_draw(streams_of[5], (D, D), 4 ** -0.5, 3.0, ((0, 2),))
    norm_mlp = jnp.clip(1.0 + 0.18 * jax.random.normal(streams_of[6], (D,), jnp.float32), 0.1, 1.9)
    w_gate = bell_draw(streams_of[7], (D, FF), D ** -0.5, 0.1875, ((0, 2),))
    w_up = bell_draw(streams_of[8], (D, FF), D ** -0.5, 0.1875, ((0, 2),))
    w_down = bell_draw(streams_of[9], (FF, D), FF ** -0.5, 0.078125, ((0, 2),))
    return {"block_input": block_input, "cotangent": cotangent, "norm_attn": norm_attn, "w_qkv": w_qkv, "b_qkv": b_qkv, "w_out": w_out, "norm_mlp": norm_mlp, "w_gate": w_gate, "w_up": w_up, "w_down": w_down}


EPSILON = 1e-06
THETA = 1000000.0

def to_narrow(value):
    return lax.optimization_barrier(value.astype(jnp.bfloat16))

def positions_of(shard, within, tok_rows, length):
    half_rows = tok_rows // 2
    return jnp.where(within < half_rows, shard * half_rows + within, length - (shard + 2) * half_rows + within).astype(jnp.int32)

def rope_tables(pos_rows, head_size):
    steps_idx = jnp.arange(head_size // 2, dtype=jnp.float32)
    inverse = THETA ** (-2.0 * steps_idx / head_size)
    angles = pos_rows.astype(jnp.float32)[:, None] * inverse[None, :]
    cosine = jnp.concatenate([jnp.cos(angles), jnp.cos(angles)], axis=1)
    sine_table = jnp.concatenate([jnp.sin(angles), jnp.sin(angles)], axis=1)
    return (cosine, sine_table)

def rotate_half(vector):
    half_size = vector.shape[-1] // 2
    return jnp.concatenate([-vector[..., half_size:], vector[..., :half_size]], axis=-1)

def rotate_back(vector):
    half_size = vector.shape[-1] // 2
    return jnp.concatenate([vector[..., half_size:], -vector[..., :half_size]], axis=-1)

def apply_rope(vector, cosine, sine_table):
    return vector * cosine[:, None, :] + rotate_half(vector) * sine_table[:, None, :]

def undo_rope(grad_vec, cosine, sine_table):
    return grad_vec * cosine[:, None, :] + rotate_back(grad_vec * sine_table[:, None, :])

def rms_norm(hidden, gain):
    inverse = lax.rsqrt(lax.optimization_barrier(jnp.mean(hidden * hidden, axis=-1, keepdims=True)) + EPSILON)
    return (hidden * inverse * gain, inverse)

def norm_back(grad_normed, hidden, inverse, gain):
    scaled = grad_normed * gain
    return inverse * (scaled - hidden * inverse * inverse * lax.optimization_barrier(jnp.mean(scaled * hidden, axis=-1, keepdims=True)))

def reference(block_input, cotangent, norm_attn, w_qkv, b_qkv, w_out, norm_mlp, w_gate, w_up, w_down):
    groups = H // KVH
    score_scale = 1.0 / math.sqrt(HD)
    q_block = math.gcd(LENGTH, 512)
    nblocks = LENGTH // q_block
    rows_all = jnp.arange(LENGTH, dtype=jnp.int32)
    pos_rows = positions_of(rows_all // TOK_DEV, rows_all % TOK_DEV, TOK_DEV, LENGTH)
    cosine, sine_table = rope_tables(pos_rows, HD)
    grad_gain1 = jnp.zeros((D,), jnp.float32)
    grad_gain2 = jnp.zeros((D,), jnp.float32)
    grad_qkv = jnp.zeros((D, QKV), jnp.float32)
    grad_bias = jnp.zeros((QKV,), jnp.float32)
    grad_wout = jnp.zeros((D, D), jnp.float32)
    grad_gate_w = jnp.zeros((D, FF), jnp.float32)
    grad_up_w = jnp.zeros((D, FF), jnp.float32)
    grad_down_w = jnp.zeros((FF, D), jnp.float32)
    outputs_y = []
    outputs_dx = []
    for seq_index in range(SEQS):
        inputs = block_input[seq_index].astype(jnp.float32)
        normed_attn, inv_attn = rms_norm(inputs, norm_attn)
        normed_attn_bf = to_narrow(normed_attn)
        project = jnp.dot(normed_attn_bf, w_qkv, preferred_element_type=jnp.float32) + b_qkv
        queries = to_narrow(apply_rope(project[:, :D].reshape(LENGTH, H, HD), cosine, sine_table))
        key_rot = to_narrow(apply_rope(project[:, D:D + KVH * HD].reshape(LENGTH, KVH, HD), cosine, sine_table))
        values = to_narrow(project[:, D + KVH * HD:].reshape(LENGTH, KVH, HD))
        keys_wide = key_rot.astype(jnp.float32)
        values_wide = values.astype(jnp.float32)

        def block_scores(block_index):
            start = block_index * q_block
            q_rows = lax.dynamic_slice_in_dim(queries, start, q_block, 0).astype(jnp.float32).reshape(q_block, KVH, groups, HD)
            q_pos = lax.dynamic_slice_in_dim(pos_rows, start, q_block, 0)
            scores = jnp.einsum('tkgd,skd->tkgs', q_rows, keys_wide) * score_scale
            allowed = (pos_rows[None, :] <= q_pos[:, None])[:, None, None, :]
            return (q_rows, scores, allowed, start)

        def forward_block(block_index):
            q_rows, scores, allowed, start = block_scores(block_index)
            masked = jnp.where(allowed, scores, -1e+30)
            run_top = lax.optimization_barrier(jnp.max(masked, axis=-1, keepdims=True))
            run_total = lax.optimization_barrier(jnp.sum(jnp.where(allowed, jnp.exp(masked - run_top), 0.0), axis=-1, keepdims=True))
            log_sum = run_top + jnp.log(run_total)
            prob_bf = to_narrow(jnp.where(allowed, jnp.exp(masked - log_sum), 0.0))
            mixed_rows = jnp.einsum('tkgs,skd->tkgd', prob_bf.astype(jnp.float32), values_wide)
            return (log_sum[..., 0], to_narrow(mixed_rows.reshape(q_block, D)))
        log_sums, attended = lax.map(forward_block, jnp.arange(nblocks))
        log_sums = log_sums.reshape(LENGTH, KVH, groups)
        attended = attended.reshape(LENGTH, D)
        hidden1 = inputs + jnp.dot(attended, w_out, preferred_element_type=jnp.float32)
        normed_mlp, inv_mlp = rms_norm(hidden1, norm_mlp)
        normed_mlp_bf = to_narrow(normed_mlp)
        gate_act = jnp.dot(normed_mlp_bf, w_gate, preferred_element_type=jnp.float32)
        up_act = jnp.dot(normed_mlp_bf, w_up, preferred_element_type=jnp.float32)
        gate_sig = jax.nn.sigmoid(gate_act)
        active = to_narrow(gate_act * gate_sig * up_act)
        output = hidden1 + jnp.dot(active, w_down, preferred_element_type=jnp.float32)
        outputs_y.append(output.astype(jnp.bfloat16))
        grad_out = cotangent[seq_index]
        grad_down_w = grad_down_w + jnp.dot(active.T, grad_out, preferred_element_type=jnp.float32)
        grad_act = jnp.dot(grad_out, w_down.T, preferred_element_type=jnp.float32)
        grad_gate_bf = to_narrow(grad_act * up_act * gate_sig * (1.0 + gate_act * (1.0 - gate_sig)))
        grad_up_bf = to_narrow(grad_act * gate_act * gate_sig)
        grad_gate_w = grad_gate_w + jnp.dot(normed_mlp_bf.T, grad_gate_bf, preferred_element_type=jnp.float32)
        grad_up_w = grad_up_w + jnp.dot(normed_mlp_bf.T, grad_up_bf, preferred_element_type=jnp.float32)
        grad_norm2 = jnp.dot(grad_gate_bf, w_gate.T, preferred_element_type=jnp.float32) + jnp.dot(grad_up_bf, w_up.T, preferred_element_type=jnp.float32)
        grad_gain2 = grad_gain2 + lax.optimization_barrier(jnp.sum(grad_norm2 * hidden1 * inv_mlp, axis=0))
        grad_hidden = grad_out.astype(jnp.float32) + norm_back(grad_norm2, hidden1, inv_mlp, norm_mlp)
        grad_hidden_bf = to_narrow(grad_hidden)
        grad_wout = grad_wout + jnp.dot(attended.T, grad_hidden_bf, preferred_element_type=jnp.float32)
        grad_attended = to_narrow(jnp.dot(grad_hidden_bf, w_out.T, preferred_element_type=jnp.float32))

        def backward_block(state_pair, block_index):
            grad_keys, grad_values = state_pair
            q_rows, scores, allowed, start = block_scores(block_index)
            grad_rows = lax.dynamic_slice_in_dim(grad_attended, start, q_block, 0).astype(jnp.float32).reshape(q_block, KVH, groups, HD)
            out_rows = lax.dynamic_slice_in_dim(attended, start, q_block, 0).astype(jnp.float32).reshape(q_block, KVH, groups, HD)
            sums_rows = lax.dynamic_slice_in_dim(log_sums, start, q_block, 0)
            row_delta = lax.optimization_barrier(jnp.sum(grad_rows * out_rows, axis=-1))
            prob_wide = jnp.where(allowed, jnp.exp(jnp.where(allowed, scores, -1e+30) - sums_rows[..., None]), 0.0)
            prob_bf = to_narrow(prob_wide).astype(jnp.float32)
            grad_values = grad_values + jnp.einsum('tkgs,tkgd->skd', prob_bf, grad_rows)
            grad_probs = jnp.einsum('tkgd,skd->tkgs', grad_rows, values_wide)
            grad_scores = to_narrow(prob_wide * (grad_probs - row_delta[..., None]) * score_scale).astype(jnp.float32)
            grad_q = jnp.einsum('tkgs,skd->tkgd', grad_scores, keys_wide)
            grad_keys = grad_keys + jnp.einsum('tkgs,tkgd->skd', grad_scores, q_rows)
            return ((grad_keys, grad_values), grad_q.reshape(q_block, H, HD))
        zero_kv = jnp.zeros((LENGTH, KVH, HD), jnp.float32)
        (grad_keys, grad_values), grad_queries = lax.scan(backward_block, (zero_kv, zero_kv), jnp.arange(nblocks))
        grad_queries = grad_queries.reshape(LENGTH, H, HD)
        grad_proj = jnp.concatenate([undo_rope(grad_queries, cosine, sine_table).reshape(LENGTH, D), undo_rope(grad_keys, cosine, sine_table).reshape(LENGTH, KVH * HD), grad_values.reshape(LENGTH, KVH * HD)], axis=1)
        grad_bias = grad_bias + lax.optimization_barrier(jnp.sum(grad_proj, axis=0))
        grad_proj_bf = to_narrow(grad_proj)
        grad_qkv = grad_qkv + jnp.dot(normed_attn_bf.T, grad_proj_bf, preferred_element_type=jnp.float32)
        grad_norm1 = jnp.dot(grad_proj_bf, w_qkv.T, preferred_element_type=jnp.float32)
        grad_gain1 = grad_gain1 + lax.optimization_barrier(jnp.sum(grad_norm1 * inputs * inv_attn, axis=0))
        outputs_dx.append(grad_hidden + norm_back(grad_norm1, inputs, inv_attn, norm_attn))
    factor = 1.0 / math.sqrt(SEQS * LENGTH)
    split_at = D + KVH * HD
    return (jnp.stack(outputs_y), jnp.stack(outputs_dx), grad_gain1 * factor, grad_qkv * factor, grad_bias[:split_at] * factor, grad_bias[split_at:] * factor, grad_wout * factor, grad_gain2 * factor, grad_gate_w * factor, grad_up_w * factor, grad_down_w * factor)
```

```python
import functools
import math

import jax
import jax.numpy as jnp
from jax import lax
from jax.experimental import pallas as pl
from jax.experimental.pallas import tpu as pltpu
from jax.sharding import PartitionSpec as P

H = 14
KVH = 2
HD = 64
EPSILON = 1e-06
THETA = 1000000.0
F32 = jnp.float32
BF = jnp.bfloat16


def rms_norm(hidden, gain):
    inverse = lax.rsqrt(jnp.mean(hidden * hidden, axis=-1, keepdims=True) + EPSILON)
    return (hidden * inverse * gain, inverse)


def norm_back(grad_normed, hidden, inverse, gain):
    scaled = grad_normed * gain
    return inverse * (
        scaled - hidden * inverse * inverse * jnp.mean(scaled * hidden, axis=-1, keepdims=True)
    )


def dot(a, b, ca=1, cb=0, out=F32):
    return lax.dot_general(a, b, (((ca,), (cb,)), ((), ())), preferred_element_type=out)


def kdot(a, b, ca, cb, precision=None):
    return lax.dot_general(
        a, b, (((ca,), (cb,)), ((), ())), preferred_element_type=F32, precision=precision
    )


def head_rows(ref, sel, head, blk):
    return ref[sel * blk : (sel + 1) * blk, head * HD : (head + 1) * HD]


def diag_mask(blk, groups, flip):
    shape = (blk, groups * blk)
    key = lax.broadcasted_iota(jnp.int32, shape, 0)
    query = lax.broadcasted_iota(jnp.int32, shape, 1) % blk
    half = blk // 2
    key = jnp.where(flip, (key + half) % blk, key)
    query = jnp.where(flip, (query + half) % blk, query)
    return key <= query


def fwd_kernel(pairs, groups, blk, idx_ref, q_ref, *refs):
    kv_refs = refs[:pairs]
    att_ref, lse_ref, kv_all, qp, scores, acc = refs[pairs:]
    here = idx_ref[0]
    core = idx_ref[1]
    width = groups * blk
    for k in range(pairs):
        kv_all[k] = kv_refs[k][...]
    zeros = jnp.zeros((blk, HD), BF)
    for sel in range(2):
        for head in range(groups):
            qp[sel, head * blk : (head + 1) * blk, :] = jnp.concatenate(
                [head_rows(q_ref, sel, head, blk), zeros], axis=1
            )

    def kv_block(low_high, j):
        return kv_all[j ^ here, pl.ds(pl.multiple_of(low_high * blk, blk), blk), :]

    def fold(top, s):
        return jnp.maximum(top, jnp.max(s.reshape(blk // 8, 8, width), axis=0))

    start = jnp.full((8, width), -1e30, F32)

    def full_step(j, top):
        s = kdot(kv_block(0, j), qp[1], 1, 1)
        scores[j] = s
        return fold(top, s)

    top_high = lax.fori_loop(0, pairs, full_step, start)

    def off_step(u, tops):
        low = u < here
        j = jnp.where(low, u, u + 1)
        sel = jnp.where(low, 0, 1)
        s = kdot(kv_block(sel, j), qp[sel], 1, 1)
        scores[pairs + u] = s
        m = jnp.max(s.reshape(blk // 8, 8, width), axis=0)
        return (
            jnp.where(low, jnp.maximum(tops[0], m), tops[0]),
            jnp.where(low, tops[1], jnp.maximum(tops[1], m)),
        )

    tops = lax.fori_loop(0, pairs - 1, off_step, (start, top_high))
    tops = list(tops)
    for sel in range(2):
        mask = diag_mask(blk, groups, (core == 1) if sel == 0 else (core == 0))
        s = jnp.where(mask, kdot(kv_block(sel, here), qp[sel], 1, 1), -1e30)
        scores[2 * pairs - 1 + sel] = s
        tops[sel] = jnp.max(fold(tops[sel], s), axis=0, keepdims=True)

    def probs(s, top):
        p = jnp.exp(s - top)
        return p.astype(BF), jnp.sum(p.reshape(blk // 8, 8, width), axis=0)

    totals = []
    for sel in range(2):
        pb, t = probs(scores[2 * pairs - 1 + sel], tops[sel])
        acc[sel] = kdot(kv_block(sel, here), pb, 0, 0)
        totals.append(t)

    def full_mix(j, total):
        pb, t = probs(scores[j], tops[1])
        acc[1] += kdot(kv_block(0, j), pb, 0, 0)
        return total + t

    totals[1] = lax.fori_loop(0, pairs, full_mix, totals[1])

    def off_mix(u, totals):
        low = u < here
        j = jnp.where(low, u, u + 1)
        sel = jnp.where(low, 0, 1)
        pb, t = probs(scores[pairs + u], jnp.where(low, tops[0], tops[1]))
        acc[sel] += kdot(kv_block(sel, j), pb, 0, 0)
        return (
            jnp.where(low, totals[0] + t, totals[0]),
            jnp.where(low, totals[1], totals[1] + t),
        )

    totals = lax.fori_loop(0, pairs - 1, off_mix, tuple(totals))
    for sel in range(2):
        total = jnp.sum(totals[sel], axis=0, keepdims=True)
        lse_ref[sel] = tops[sel] + jnp.log(total)
        mixed = acc[sel, HD:, :] / total
        for head in range(groups):
            att_ref[sel * blk : (sel + 1) * blk, head * HD : (head + 1) * HD] = (
                mixed[:, head * blk : (head + 1) * blk].T.astype(BF)
            )


def bwd_kernel(pairs, groups, blk, scale, idx_ref, q_ref, do_ref, att_ref, lse_ref, *refs):
    kv_refs = refs[:pairs]
    dq_ref = refs[pairs]
    dkv_refs = refs[pairs + 1 : 2 * pairs + 1]
    kv_all, qp, dop, dkv, dq_acc = refs[2 * pairs + 1 :]
    here = idx_ref[0]
    core = idx_ref[1]
    width = groups * blk
    for k in range(pairs):
        kv_all[k] = kv_refs[k][...]
    zeros = jnp.zeros((blk, HD), BF)
    for sel in range(2):
        for head in range(groups):
            rows = slice(head * blk, (head + 1) * blk)
            qp[sel, rows, :] = jnp.concatenate([head_rows(q_ref, sel, head, blk), zeros], axis=1)
            dop[sel, rows, :] = jnp.concatenate([zeros, head_rows(do_ref, sel, head, blk)], axis=1)
    prod = do_ref[...].astype(F32) * att_ref[...].astype(F32)
    picks_shape = (8, groups * HD)
    picks = (
        lax.broadcasted_iota(jnp.int32, picks_shape, 1) // HD
        == lax.broadcasted_iota(jnp.int32, picks_shape, 0)
    ).astype(F32)
    delta_heads = kdot(picks, prod, 1, 1, lax.Precision.HIGHEST)
    deltas = [
        jnp.concatenate(
            [delta_heads[h : h + 1, sel * blk : (sel + 1) * blk] for h in range(groups)], axis=1
        )
        for sel in range(2)
    ]
    lses = [lse_ref[0], lse_ref[1]]

    def kv_block(low_high, j):
        return kv_all[j ^ here, pl.ds(pl.multiple_of(low_high * blk, blk), blk), :]

    def terms(kv, sel, lse, delta, mask=None):
        s = kdot(kv, qp[sel], 1, 1)
        p = jnp.exp(s - lse) if mask is None else jnp.where(
            mask, jnp.exp(jnp.where(mask, s, -1e30) - lse), 0.0
        )
        dp = kdot(kv, dop[sel], 1, 1)
        ds = (p * (dp - delta)).astype(BF)
        pb = p.astype(BF)
        dk = kdot(ds, qp[sel], 1, 0) + kdot(pb, dop[sel], 1, 0)
        return ds, dk

    for sel in range(2):
        mask = diag_mask(blk, groups, (core == 1) if sel == 0 else (core == 0))
        kv = kv_block(sel, here)
        ds, dk = terms(kv, sel, lses[sel], deltas[sel], mask)
        dq_acc[sel] = kdot(kv, ds, 0, 0)
        dkv[here, sel] = dk
        if sel == 0:
            dkv_low_here = dk

    def full_step(j, carry):
        kv = kv_block(0, j)
        ds, dk = terms(kv, 1, lses[1], deltas[1])
        dq_acc[1] += kdot(kv, ds, 0, 0)

        @pl.when(j == here)
        def _():
            dkv[j, 0] += dk

        @pl.when(j != here)
        def _():
            dkv[j, 0] = dk

        return carry

    lax.fori_loop(0, pairs, full_step, 0)

    def off_step(u, carry):
        low = u < here
        j = jnp.where(low, u, u + 1)
        sel = jnp.where(low, 0, 1)
        kv = kv_block(sel, j)
        ds, dk = terms(
            kv, sel, jnp.where(low, lses[0], lses[1]), jnp.where(low, deltas[0], deltas[1])
        )
        dq_acc[sel] += kdot(kv, ds, 0, 0)

        @pl.when(low)
        def _():
            dkv[j, 0] += dk
            dkv[j, 1] = jnp.zeros_like(dk)

        @pl.when(jnp.logical_not(low))
        def _():
            dkv[j, 1] = dk

        return carry

    lax.fori_loop(0, pairs - 1, off_step, 0)
    for k in range(pairs):
        for sel in range(2):
            dkv_refs[k][sel * blk : (sel + 1) * blk, :] = dkv[k ^ here, sel].astype(
                dkv_refs[k].dtype
            )
    for sel in range(2):
        for head in range(groups):
            dq_ref[sel * blk : (sel + 1) * blk, head * HD : (head + 1) * HD] = (
                dq_acc[sel, :HD, head * blk : (head + 1) * blk].T * scale
            )


VMEM_SPEC = pl.BlockSpec(memory_space=pltpu.VMEM)
SMEM_SPEC = pl.BlockSpec(memory_space=pltpu.SMEM)


def attention_fwd(idx, q, kvs):
    pairs = len(kvs)
    rows, cols = q.shape
    blk = rows // 2
    groups = cols // HD
    width = groups * blk
    return pl.pallas_call(
        functools.partial(fwd_kernel, pairs, groups, blk),
        out_shape=(
            jax.ShapeDtypeStruct((rows, cols), BF),
            jax.ShapeDtypeStruct((2, 1, width), F32),
        ),
        in_specs=[SMEM_SPEC] + [VMEM_SPEC] * (1 + pairs),
        out_specs=(VMEM_SPEC, VMEM_SPEC),
        scratch_shapes=[
            pltpu.VMEM((pairs, rows, 2 * HD), BF),
            pltpu.VMEM((2, width, 2 * HD), BF),
            pltpu.VMEM((2 * pairs + 1, blk, width), F32),
            pltpu.VMEM((2, 2 * HD, width), F32),
        ],
        compiler_params=pltpu.CompilerParams(vmem_limit_bytes=56 * 2**20),
        name="attn_fwd",
    )(idx, q, *kvs)


def attention_bwd(idx, q, d_out, att, lse, kvs):
    pairs = len(kvs)
    rows, cols = q.shape
    blk = rows // 2
    groups = cols // HD
    width = groups * blk
    res = pl.pallas_call(
        functools.partial(bwd_kernel, pairs, groups, blk, 1.0 / math.sqrt(HD)),
        out_shape=(jax.ShapeDtypeStruct((rows, cols), F32),)
        + tuple(jax.ShapeDtypeStruct((rows, 2 * HD), BF) for _ in range(pairs)),
        in_specs=[SMEM_SPEC] + [VMEM_SPEC] * (4 + pairs),
        out_specs=(VMEM_SPEC,) * (1 + pairs),
        scratch_shapes=[
            pltpu.VMEM((pairs, rows, 2 * HD), BF),
            pltpu.VMEM((2, width, 2 * HD), BF),
            pltpu.VMEM((2, width, 2 * HD), BF),
            pltpu.VMEM((pairs, 2, blk, 2 * HD), F32),
            pltpu.VMEM((2, 2 * HD, width), F32),
        ],
        compiler_params=pltpu.CompilerParams(vmem_limit_bytes=56 * 2**20),
        name="attn_bwd",
    )(idx, q, d_out, att, lse, *kvs)
    return res[0], res[1:]


def shards(block_input, cotangent, norm_attn, w_qkv, b_qkv, w_out, norm_mlp, w_gate, w_up, w_down):
    ctx_count = lax.axis_size("ctx")
    groups_z = ctx_count // 4
    pairs = ctx_count // 2
    device_count = 2 * ctx_count
    _, tok, dim = block_input.shape
    half_tok = tok // 2
    length = tok * ctx_count
    half_dim = dim // 2
    kv_cols = KVH * HD
    ff = w_gate.shape[1]
    ff_blk = ff // device_count
    factor = 1.0 / math.sqrt(2 * length)
    ctx = lax.axis_index("ctx")
    wt = lax.axis_index("wt")
    core = ctx % 2
    chip_y = (ctx // 2) % 2
    pair = ctx // 2
    group = ctx // 4
    plane = (ctx % 4) * 2 + wt

    def swap(a, cx, wx):
        if wx == 0:
            return lax.ppermute(a, "ctx", [(i, i ^ cx) for i in range(ctx_count)])
        if cx == 0:
            return lax.ppermute(a, "wt", [(0, 1), (1, 0)])
        return lax.ppermute(
            a, ("ctx", "wt"), [(i, i ^ (2 * cx + wx)) for i in range(device_count)]
        )

    def shift(a, k):
        return lax.ppermute(a, "ctx", [(i, (i + 4 * k) % ctx_count) for i in range(ctx_count)])

    def by_bit(bit, first, second, axis):
        return jnp.where(
            bit == 0,
            jnp.concatenate([first, second], axis=axis),
            jnp.concatenate([second, first], axis=axis),
        )

    def pick(a, index, axis=0):
        return lax.dynamic_index_in_dim(a, index, axis, keepdims=False)

    def pair_rows(own, peer):
        return jnp.concatenate(
            [own[:half_tok], peer[:half_tok], own[half_tok:], peer[half_tok:]], axis=0
        )

    def own_rows(a):
        return jnp.concatenate([a[:half_tok], a[tok : tok + half_tok]], axis=0)

    def peer_rows(a):
        return jnp.concatenate([a[half_tok:tok], a[tok + half_tok :]], axis=0)

    x_own = block_input[0]
    x_two = pair_rows(x_own, swap(x_own, 1, 0)).astype(F32)
    head_cols = dim // KVH

    def core_cols(a, axis):
        pieces = [
            (head_cols * core, head_cols),
            (dim + HD * core, HD),
            (dim + kv_cols + HD * core, HD),
        ]
        return jnp.concatenate(
            [lax.dynamic_slice_in_dim(a, s, w, axis) for s, w in pieces], axis=axis
        )

    wq_own = core_cols(w_qkv, 1)
    wq = by_bit(wt, wq_own, swap(wq_own, 0, 1), 0)
    b_own = core_cols(b_qkv, 0)

    def ff_cols(a, p):
        return jnp.concatenate(
            [
                lax.dynamic_slice_in_dim(a, (g * 8 + p) * ff_blk, ff_blk, 1)
                for g in range(groups_z)
            ],
            axis=1,
        )

    def plane_gather(a):
        four = jnp.concatenate([a, swap(a, 0, 1), swap(a, 2, 0), swap(a, 2, 1)], axis=0)
        return jnp.concatenate([four, swap(four, 1, 0)], axis=0)

    def plane_scatter(part):
        half = part.shape[0] // 2
        quad = part[:half] + swap(part[half:].astype(BF), 1, 0).astype(F32)
        quad = quad.reshape(4, tok, dim)
        return (
            quad[0]
            + swap(quad[1].astype(BF), 0, 1).astype(F32)
            + swap(quad[2].astype(BF), 2, 0).astype(F32)
            + swap(quad[3].astype(BF), 2, 1).astype(F32)
        )

    wo_cols = lax.dynamic_slice_in_dim(w_out, half_dim * core, half_dim, 1)
    wo_recv = swap(wo_cols, 0, 1)
    wo_other = by_bit(core, wo_recv, swap(wo_recv, 1, 0), 1)
    wo = by_bit(wt, w_out, wo_other, 0)
    gate_w = by_bit(wt, ff_cols(w_gate, plane), swap(ff_cols(w_gate, plane ^ 1), 0, 1), 0)
    up_w = by_bit(wt, ff_cols(w_up, plane), swap(ff_cols(w_up, plane ^ 1), 0, 1), 0)
    down_blocks = w_down.reshape(groups_z // 2, 8, ff_blk, dim)
    down_w = by_bit(
        wt,
        pick(down_blocks, plane, 1).reshape(-1, dim),
        swap(pick(down_blocks, plane ^ 1, 1).reshape(-1, dim), 0, 1),
        0,
    )
    cot_own = cotangent[0]
    cot_all = plane_gather(cot_own)

    normed1, inv1 = rms_norm(x_two, norm_attn)
    normed1_bf = normed1.astype(BF)
    project = dot(normed1_bf, wq) + b_own
    within = jnp.arange(half_tok, dtype=jnp.int32)
    peer = ctx ^ 1
    pos = jnp.concatenate(
        [
            ctx * half_tok + within,
            peer * half_tok + within,
            length - (ctx + 1) * half_tok + within,
            length - (peer + 1) * half_tok + within,
        ]
    )
    steps = jnp.arange(HD // 2, dtype=F32)
    angles = pos.astype(F32)[:, None] * (THETA ** (-2.0 * steps / HD))[None, :]
    rope_cols = head_cols + HD
    cosine = jnp.tile(jnp.cos(angles), (1, 2 * rope_cols // HD))
    sine = jnp.tile(jnp.sin(angles), (1, 2 * rope_cols // HD))
    first_half = (lax.broadcasted_iota(jnp.int32, (1, rope_cols), 1) % HD) < HD // 2

    def halves(u):
        return jnp.roll(u, -(HD // 2), axis=1), jnp.roll(u, HD // 2, axis=1)

    def rope(u):
        ahead, behind = halves(u)
        return u * cosine + jnp.where(first_half, -ahead, behind) * sine

    def unrope(g):
        ahead, behind = halves(g * sine)
        return g * cosine + jnp.where(first_half, ahead, -behind)

    rotated = rope(project[:, :rope_cols]).astype(BF)
    q_scaled = rotated[:, :head_cols] * BF(1.0 / math.sqrt(HD))
    kv_own = jnp.concatenate([rotated[:, head_cols:], project[:, rope_cols:].astype(BF)], axis=1)
    kvs = [kv_own] + [swap(kv_own, 2 * k, 0) for k in range(1, pairs)]
    idx = jnp.stack([pair, core]).astype(jnp.int32)
    att_heads, lse = attention_fwd(idx, q_scaled, kvs)
    att_peer = swap(att_heads, 1, 0)
    att_peer = pair_rows(peer_rows(att_peer), own_rows(att_peer))
    att_two = by_bit(core, att_heads, att_peer, 1)
    hidden1 = x_own.astype(F32) + dot(own_rows(att_two), wo)
    normed2, inv2 = rms_norm(hidden1, norm_mlp)
    n2 = plane_gather(normed2.astype(BF))

    gate = dot(n2, gate_w)
    up = dot(n2, up_w)
    grad_act = dot(cot_all, down_w, 1, 1)
    sig = jax.nn.sigmoid(gate)
    active = (gate * sig * up).astype(BF)
    g_gate = (grad_act * up * sig * (1.0 + gate * (1.0 - sig))).astype(BF)
    g_up = (grad_act * gate * sig).astype(BF)
    grad_norm2 = plane_scatter(dot(g_gate, gate_w, 1, 1) + dot(g_up, up_w, 1, 1))
    output = (hidden1 + plane_scatter(dot(active, down_w))).astype(BF)
    gw_gate = dot(n2, g_gate, 0, 0, BF)
    gw_up = dot(n2, g_up, 0, 0, BF)
    gw_down = dot(active, cot_all, 0, 0, BF)

    gg_mlp = jnp.sum(grad_norm2 * hidden1 * inv2, axis=0)
    grad_hidden = cot_own.astype(F32) + norm_back(grad_norm2, hidden1, inv2, norm_mlp)
    gh_own = grad_hidden.astype(BF)
    gh_two = pair_rows(gh_own, swap(gh_own, 1, 0))
    wo_rows = lax.dynamic_slice_in_dim(wo, half_dim * core, half_dim, 0)
    grad_att = dot(gh_two, wo_rows, 1, 1, BF)
    gw_out = dot(att_two, lax.dynamic_slice_in_dim(gh_two, half_dim * core, half_dim, 1), 0, 0, BF)

    dq, dkvs = attention_bwd(idx, q_scaled, grad_att, att_heads, lse, kvs)
    dkv = dkvs[0].astype(F32)
    for k in range(1, pairs):
        dkv = dkv + swap(dkvs[k], 2 * k, 0).astype(F32)
    roped = unrope(jnp.concatenate([dq, dkv[:, :HD]], axis=1))
    grad_proj = jnp.concatenate([roped, dkv[:, HD:]], axis=1)
    gb = jnp.sum(grad_proj, axis=0)
    gp_bf = grad_proj.astype(BF)
    gw_qkv = dot(normed1_bf, gp_bf, 0, 0, BF)
    gn1_part = dot(gp_bf, wq, 1, 1)
    grad_norm1 = own_rows(gn1_part) + swap(peer_rows(gn1_part), 1, 0)
    x32 = x_own.astype(F32)
    inv1_own = own_rows(inv1)
    gg_attn = jnp.sum(grad_norm1 * x32 * inv1_own, axis=0)
    grad_input = grad_hidden + norm_back(grad_norm1, x32, inv1_own, norm_attn)

    def z_sum(a):
        total = pick(a, group).astype(F32)
        for k in range(1, groups_z):
            total = total + shift(pick(a, (group + k) % groups_z), k).astype(F32)
        return total

    def plane_step(a, bit, cx, wx):
        return pick(a, bit), swap(pick(a, 1 - bit), cx, wx)

    rows = dim // device_count

    def plane_collect(a):
        a = a.astype(BF).reshape(2, 2, 2, rows, -1)
        mine, other = plane_step(jnp.moveaxis(a, 1, 0), core, 1, 0)
        a = by_bit(core, mine[None], other[None], 0)
        mine, other = plane_step(jnp.moveaxis(a, 1, 0), chip_y, 2, 0)
        a = by_bit(chip_y, mine[None], other[None], 0)
        mine, other = plane_step(jnp.moveaxis(a, 2, 0), wt, 0, 1)
        a = by_bit(wt, mine[None], other[None], 0)
        return jnp.transpose(a, (1, 2, 0, 3, 4)).reshape(8, rows, -1)

    def plane_reduce(a):
        a = a.astype(BF).reshape(2, 2, 2, a.shape[0] // 8, -1)
        mine, other = plane_step(jnp.moveaxis(a, 1, 0), core, 1, 0)
        a = by_bit(core, mine, other, -1)
        mine, other = plane_step(a, chip_y, 2, 0)
        a = mine.astype(F32) + other.astype(F32)
        mine, other = plane_step(a.astype(BF), wt, 0, 1)
        return mine.astype(F32) + other.astype(F32)

    sum_gu = z_sum(jnp.concatenate([gw_gate, gw_up], axis=1).reshape(groups_z, dim // groups_z, -1))
    shard_down = z_sum(gw_down.reshape(groups_z, ff_blk, dim)) * factor
    sum_out = z_sum(gw_out.reshape(groups_z, dim // groups_z, -1))
    parts = plane_collect(sum_gu).reshape(8, rows, 2, groups_z, ff_blk).astype(F32) * factor
    shard_gate = jnp.transpose(parts[:, :, 0], (1, 2, 0, 3)).reshape(rows, ff)
    shard_up = jnp.transpose(parts[:, :, 1], (1, 2, 0, 3)).reshape(rows, ff)
    shard_wout = plane_reduce(sum_out) * factor

    zero_q = jnp.zeros((head_cols,), F32)
    zero_h = jnp.zeros((HD,), F32)
    gb_full = jnp.concatenate(
        [
            by_bit(core, gb[:head_cols], zero_q, 0),
            by_bit(core, gb[head_cols:rope_cols], zero_h, 0),
            by_bit(core, gb[rope_cols:], zero_h, 0),
        ]
    )
    split_at = dim + kv_cols
    n_qk = split_at // device_count
    n_v = kv_cols // device_count
    small = jnp.concatenate(
        [
            gg_attn.reshape(device_count, rows),
            gg_mlp.reshape(device_count, rows),
            gb_full[:split_at].reshape(device_count, n_qk),
            gb_full[split_at:].reshape(device_count, n_v),
        ],
        axis=1,
    )
    n_small = small.shape[1]
    own_cols = gw_qkv.shape[1]
    small = jnp.pad(small, ((0, 0), (0, own_cols - n_small)))
    tail = jnp.concatenate(
        [gw_qkv.reshape(device_count, rows, own_cols), small.astype(BF)[:, None, :]], axis=1
    )
    tail = z_sum(tail.reshape(groups_z, 8 * (rows + 1), own_cols))
    tail = plane_reduce(tail) * factor
    low, high = tail[:, :own_cols], tail[:, own_cols:]
    shard_qkv = jnp.concatenate(
        [
            low[:rows, :head_cols],
            high[:rows, :head_cols],
            low[:rows, head_cols:rope_cols],
            high[:rows, head_cols:rope_cols],
            low[:rows, rope_cols:],
            high[:rows, rope_cols:],
        ],
        axis=1,
    )
    vec = low[rows, :n_small] + high[rows, :n_small]
    return (
        output[None],
        grad_input[None],
        vec[:rows],
        shard_qkv,
        vec[2 * rows : 2 * rows + n_qk],
        vec[2 * rows + n_qk :],
        shard_wout,
        vec[rows : 2 * rows],
        shard_gate,
        shard_up,
        shard_down,
    )


def solution(mesh):
    both = P(("ctx", "wt"))
    both_rows = P(("ctx", "wt"), None)
    tokens = P("wt", "ctx", None)
    weight = P("wt", None)
    return jax.shard_map(
        shards,
        mesh=mesh,
        in_specs=(tokens, tokens, P(), weight, P(), weight, P(), weight, weight, weight),
        out_specs=(
            tokens,
            tokens,
            both,
            both_rows,
            both,
            both,
            both_rows,
            both,
            both_rows,
            both_rows,
            both_rows,
        ),
        check_vma=False,
    )
```

```python
import functools
import math

import jax
import jax.numpy as jnp
from jax import lax
from jax.experimental import pallas as pl
from jax.experimental.pallas import tpu as pltpu
from jax.sharding import PartitionSpec as P

H = 14
KVH = 2
HD = 64
EPSILON = 1e-06
THETA = 1000000.0
F32 = jnp.float32
BF = jnp.bfloat16


def rms_norm(hidden, gain):
    inverse = lax.rsqrt(jnp.mean(hidden * hidden, axis=-1, keepdims=True) + EPSILON)
    return (hidden * inverse * gain, inverse)


def norm_back(grad_normed, hidden, inverse, gain):
    scaled = grad_normed * gain
    return inverse * (
        scaled - hidden * inverse * inverse * jnp.mean(scaled * hidden, axis=-1, keepdims=True)
    )


def after(value, done):
    return lax.optimization_barrier((value, done))[0]


def dot(a, b, ca=1, cb=0, out=F32):
    return lax.dot_general(a, b, (((ca,), (cb,)), ((), ())), preferred_element_type=out)


def kdot(a, b, ca, cb, precision=None):
    return lax.dot_general(
        a, b, (((ca,), (cb,)), ((), ())), preferred_element_type=F32, precision=precision
    )


def head_rows(ref, sel, head, blk):
    return ref[sel * blk : (sel + 1) * blk, head * HD : (head + 1) * HD]


def diag_mask(blk, groups, flip):
    shape = (blk, groups * blk)
    key = lax.broadcasted_iota(jnp.int32, shape, 0)
    query = lax.broadcasted_iota(jnp.int32, shape, 1) % blk
    half = blk // 2
    key = jnp.where(flip, (key + half) % blk, key)
    query = jnp.where(flip, (query + half) % blk, query)
    return key <= query


def fwd_kernel(pairs, groups, blk, idx_ref, q_ref, *refs):
    kv_refs = refs[:pairs]
    att_ref, lse_ref, kv_all, qp, scores, acc = refs[pairs:]
    here = idx_ref[0]
    core = idx_ref[1]
    width = groups * blk
    for k in range(pairs):
        kv_all[k] = kv_refs[k][...]
    zeros = jnp.zeros((blk, HD), BF)
    for sel in range(2):
        for head in range(groups):
            qp[sel, head * blk : (head + 1) * blk, :] = jnp.concatenate(
                [head_rows(q_ref, sel, head, blk), zeros], axis=1
            )

    def kv_block(low_high, j):
        return kv_all[j ^ here, pl.ds(pl.multiple_of(low_high * blk, blk), blk), :]

    def fold(top, s):
        return jnp.maximum(top, jnp.max(s.reshape(blk // 8, 8, width), axis=0))

    start = jnp.full((8, width), -1e30, F32)

    def full_step(j, top):
        s = kdot(kv_block(0, j), qp[1], 1, 1)
        scores[j] = s
        return fold(top, s)

    top_high = lax.fori_loop(0, pairs, full_step, start)

    def off_step(u, tops):
        low = u < here
        j = jnp.where(low, u, u + 1)
        sel = jnp.where(low, 0, 1)
        s = kdot(kv_block(sel, j), qp[sel], 1, 1)
        scores[pairs + u] = s
        m = jnp.max(s.reshape(blk // 8, 8, width), axis=0)
        return (
            jnp.where(low, jnp.maximum(tops[0], m), tops[0]),
            jnp.where(low, tops[1], jnp.maximum(tops[1], m)),
        )

    tops = lax.fori_loop(0, pairs - 1, off_step, (start, top_high))
    tops = list(tops)
    for sel in range(2):
        mask = diag_mask(blk, groups, (core == 1) if sel == 0 else (core == 0))
        s = jnp.where(mask, kdot(kv_block(sel, here), qp[sel], 1, 1), -1e30)
        scores[2 * pairs - 1 + sel] = s
        tops[sel] = jnp.max(fold(tops[sel], s), axis=0, keepdims=True)

    def probs(s, top):
        p = jnp.exp(s - top)
        return p.astype(BF), jnp.sum(p.reshape(blk // 8, 8, width), axis=0)

    totals = []
    for sel in range(2):
        pb, t = probs(scores[2 * pairs - 1 + sel], tops[sel])
        acc[sel] = kdot(kv_block(sel, here), pb, 0, 0)
        totals.append(t)

    def full_mix(j, total):
        pb, t = probs(scores[j], tops[1])
        acc[1] += kdot(kv_block(0, j), pb, 0, 0)
        return total + t

    totals[1] = lax.fori_loop(0, pairs, full_mix, totals[1])

    def off_mix(u, totals):
        low = u < here
        j = jnp.where(low, u, u + 1)
        sel = jnp.where(low, 0, 1)
        pb, t = probs(scores[pairs + u], jnp.where(low, tops[0], tops[1]))
        acc[sel] += kdot(kv_block(sel, j), pb, 0, 0)
        return (
            jnp.where(low, totals[0] + t, totals[0]),
            jnp.where(low, totals[1], totals[1] + t),
        )

    totals = lax.fori_loop(0, pairs - 1, off_mix, tuple(totals))
    for sel in range(2):
        total = jnp.sum(totals[sel], axis=0, keepdims=True)
        lse_ref[sel] = tops[sel] + jnp.log(total)
        mixed = acc[sel, HD:, :] / total
        for head in range(groups):
            att_ref[sel * blk : (sel + 1) * blk, head * HD : (head + 1) * HD] = (
                mixed[:, head * blk : (head + 1) * blk].T.astype(BF)
            )


def bwd_kernel(
    pairs, groups, blk, scale, idx_ref, q_ref, do_ref, att_ref, lse_ref, rope_ref, *refs
):
    kv_refs = refs[:pairs]
    gq_ref, gsum_ref = refs[pairs : pairs + 2]
    dkv_refs = refs[pairs + 2 : 2 * pairs + 2]
    kv_all, qp, dop, dkv, dq_acc = refs[2 * pairs + 2 :]
    here = idx_ref[0]
    core = idx_ref[1]
    width = groups * blk
    for k in range(pairs):
        kv_all[k] = kv_refs[k][...]
    zeros = jnp.zeros((blk, HD), BF)
    for sel in range(2):
        for head in range(groups):
            rows = slice(head * blk, (head + 1) * blk)
            qp[sel, rows, :] = jnp.concatenate([head_rows(q_ref, sel, head, blk), zeros], axis=1)
            dop[sel, rows, :] = jnp.concatenate([zeros, head_rows(do_ref, sel, head, blk)], axis=1)
    prod = do_ref[...].astype(F32) * att_ref[...].astype(F32)
    picks_shape = (8, groups * HD)
    picks = (
        lax.broadcasted_iota(jnp.int32, picks_shape, 1) // HD
        == lax.broadcasted_iota(jnp.int32, picks_shape, 0)
    ).astype(F32)
    delta_heads = kdot(picks, prod, 1, 1, lax.Precision.HIGHEST)
    deltas = [
        jnp.concatenate(
            [delta_heads[h : h + 1, sel * blk : (sel + 1) * blk] for h in range(groups)], axis=1
        )
        for sel in range(2)
    ]
    lses = [lse_ref[0], lse_ref[1]]

    def kv_block(low_high, j):
        return kv_all[j ^ here, pl.ds(pl.multiple_of(low_high * blk, blk), blk), :]

    def terms(kv, sel, lse, delta, mask=None):
        s = kdot(kv, qp[sel], 1, 1)
        p = jnp.exp(s - lse) if mask is None else jnp.where(
            mask, jnp.exp(jnp.where(mask, s, -1e30) - lse), 0.0
        )
        dp = kdot(kv, dop[sel], 1, 1)
        ds = (p * (dp - delta)).astype(BF)
        pb = p.astype(BF)
        dk = kdot(ds, qp[sel], 1, 0) + kdot(pb, dop[sel], 1, 0)
        return ds, dk

    for sel in range(2):
        mask = diag_mask(blk, groups, (core == 1) if sel == 0 else (core == 0))
        kv = kv_block(sel, here)
        ds, dk = terms(kv, sel, lses[sel], deltas[sel], mask)
        dq_acc[sel] = kdot(kv, ds, 0, 0)
        dkv[here, sel] = dk
        if sel == 0:
            dkv_low_here = dk

    def full_step(j, carry):
        kv = kv_block(0, j)
        ds, dk = terms(kv, 1, lses[1], deltas[1])
        dq_acc[1] += kdot(kv, ds, 0, 0)

        @pl.when(j == here)
        def _():
            dkv[j, 0] += dk

        @pl.when(j != here)
        def _():
            dkv[j, 0] = dk

        return carry

    lax.fori_loop(0, pairs, full_step, 0)

    def off_step(u, carry):
        low = u < here
        j = jnp.where(low, u, u + 1)
        sel = jnp.where(low, 0, 1)
        kv = kv_block(sel, j)
        ds, dk = terms(
            kv, sel, jnp.where(low, lses[0], lses[1]), jnp.where(low, deltas[0], deltas[1])
        )
        dq_acc[sel] += kdot(kv, ds, 0, 0)

        @pl.when(low)
        def _():
            dkv[j, 0] += dk
            dkv[j, 1] = jnp.zeros_like(dk)

        @pl.when(jnp.logical_not(low))
        def _():
            dkv[j, 1] = dk

        return carry

    lax.fori_loop(0, pairs - 1, off_step, 0)
    for k in range(pairs):
        for sel in range(2):
            dkv_refs[k][sel * blk : (sel + 1) * blk, :] = dkv[k ^ here, sel].astype(
                dkv_refs[k].dtype
            )
    for head in range(groups):
        cols = slice(head * HD, (head + 1) * HD)
        total = jnp.zeros((1, HD), F32)
        for sel in range(2):
            rows = slice(sel * blk, (sel + 1) * blk)
            cosine = rope_ref[0, :, rows]
            sine = rope_ref[1, :, rows]
            turned = dq_acc[sel, :HD, head * blk : (head + 1) * blk] * scale
            low, high = turned[: HD // 2], turned[HD // 2 :]
            back = jnp.concatenate(
                [low * cosine + high * sine, high * cosine - low * sine], axis=0
            ).T
            gq_ref[rows, cols] = back.astype(BF)
            total = total + jnp.sum(back, axis=0, keepdims=True)
        gsum_ref[:, cols] = total


VMEM_SPEC = pl.BlockSpec(memory_space=pltpu.VMEM)
SMEM_SPEC = pl.BlockSpec(memory_space=pltpu.SMEM)


def attention_fwd(idx, q, kvs):
    pairs = len(kvs)
    rows, cols = q.shape
    blk = rows // 2
    groups = cols // HD
    width = groups * blk
    return pl.pallas_call(
        functools.partial(fwd_kernel, pairs, groups, blk),
        out_shape=(
            jax.ShapeDtypeStruct((rows, cols), BF),
            jax.ShapeDtypeStruct((2, 1, width), F32),
        ),
        in_specs=[SMEM_SPEC] + [VMEM_SPEC] * (1 + pairs),
        out_specs=(VMEM_SPEC, VMEM_SPEC),
        scratch_shapes=[
            pltpu.VMEM((pairs, rows, 2 * HD), BF),
            pltpu.VMEM((2, width, 2 * HD), BF),
            pltpu.VMEM((2 * pairs + 1, blk, width), F32),
            pltpu.VMEM((2, 2 * HD, width), F32),
        ],
        compiler_params=pltpu.CompilerParams(vmem_limit_bytes=56 * 2**20),
        name="attn_fwd",
    )(idx, q, *kvs)


def attention_bwd(idx, q, d_out, att, lse, rope_t, kvs):
    pairs = len(kvs)
    rows, cols = q.shape
    blk = rows // 2
    groups = cols // HD
    width = groups * blk
    res = pl.pallas_call(
        functools.partial(bwd_kernel, pairs, groups, blk, 1.0 / math.sqrt(HD)),
        out_shape=(jax.ShapeDtypeStruct((rows, cols), BF), jax.ShapeDtypeStruct((1, cols), F32))
        + tuple(jax.ShapeDtypeStruct((rows, 2 * HD), BF) for _ in range(pairs)),
        in_specs=[SMEM_SPEC] + [VMEM_SPEC] * (5 + pairs),
        out_specs=(VMEM_SPEC,) * (2 + pairs),
        scratch_shapes=[
            pltpu.VMEM((pairs, rows, 2 * HD), BF),
            pltpu.VMEM((2, width, 2 * HD), BF),
            pltpu.VMEM((2, width, 2 * HD), BF),
            pltpu.VMEM((pairs, 2, blk, 2 * HD), F32),
            pltpu.VMEM((2, 2 * HD, width), F32),
        ],
        compiler_params=pltpu.CompilerParams(vmem_limit_bytes=56 * 2**20),
        name="attn_bwd",
    )(idx, q, d_out, att, lse, rope_t, *kvs)
    return res[0], res[1], res[2:]


def columns_kernel(groups_z, ff_blk, ff_wide, window, idx_ref, gate_ref, up_ref, out_ref, win, sems):
    ff = gate_ref.shape[1]
    here = idx_ref[0]
    shifts = []
    copies = []
    for m, ref in enumerate((gate_ref, up_ref)):
        for g in range(groups_z):
            col = (g * 8 + here) * ff_blk
            start = jnp.minimum((col // 128) * 128, ff - window)
            if m == 0:
                shifts.append(col - start)
            copies.append(
                pltpu.make_async_copy(
                    ref.at[:, pl.ds(pl.multiple_of(start, 128), window)],
                    win.at[m * groups_z + g],
                    sems.at[m * groups_z + g],
                )
            )
    for copy in copies:
        copy.start()
    for m in range(2):
        pieces = [None] * (ff_wide // 128)
        for g in range(groups_z):
            first = g * ff_blk // 128
            lead = g * ff_blk - first * 128
            tiles = -(-(lead + ff_blk) // 128)
            copies[m * groups_z + g].wait()
            row = lax.broadcasted_iota(jnp.int32, (window, tiles * 128), 0)
            lane = lax.broadcasted_iota(jnp.int32, (window, tiles * 128), 1) - lead
            hot = jnp.logical_and(row == lane + shifts[g], jnp.logical_and(lane >= 0, lane < ff_blk))
            part = kdot(win[m * groups_z + g], hot.astype(F32).astype(BF), 1, 0)
            for t in range(tiles):
                tile = part[:, t * 128 : (t + 1) * 128]
                old = pieces[first + t]
                pieces[first + t] = tile if old is None else old + tile
        for t, tile in enumerate(pieces):
            col = m * ff_wide + t * 128
            out_ref[:, col : col + 128] = (
                jnp.zeros((out_ref.shape[0], 128), BF) if tile is None else tile.astype(BF)
            )


def hidden_columns(idx, gate, up, groups_z, ff_blk, ff_wide):
    rows, ff = gate.shape
    window = min(-(-(ff_blk + 127) // 128) * 128, ff)
    return pl.pallas_call(
        functools.partial(columns_kernel, groups_z, ff_blk, ff_wide, window),
        out_shape=jax.ShapeDtypeStruct((rows, 2 * ff_wide), BF),
        in_specs=[SMEM_SPEC, pl.BlockSpec(memory_space=pl.ANY), pl.BlockSpec(memory_space=pl.ANY)],
        out_specs=VMEM_SPEC,
        scratch_shapes=[
            pltpu.VMEM((2 * groups_z, rows, window), BF),
            pltpu.SemaphoreType.DMA((2 * groups_z,)),
        ],
        name="hidden_columns",
    )(idx, gate, up)


def mlp_kernel(idx_ref, *refs):
    n2_refs, cot_refs = refs[:8], refs[8:16]
    gu_own, gu_recv, down_own, down_recv = refs[16:20]
    keep_ref, send_ref, g_ref, act_ref, n2_all, cot_all, down_w = refs[20:27]
    gu_w = refs[27]
    wt = idx_ref[0]
    tok = n2_refs[0].shape[0]
    half = gu_own.shape[0]
    down_half = down_own.shape[0]
    wide = gu_own.shape[1] // 2
    for k in range(8):
        n2_all[k * tok : (k + 1) * tok, :] = n2_refs[k][...]
        cot_all[k * tok : (k + 1) * tok, :] = cot_refs[k][...]
    gu_w[pl.ds(pl.multiple_of(wt * half, 16), half), :] = gu_own[...]
    gu_w[pl.ds(pl.multiple_of((1 - wt) * half, 16), half), :] = gu_recv[...]
    down_w[pl.ds(pl.multiple_of(wt * down_half, 16), down_half), :] = down_own[...]
    down_w[pl.ds(pl.multiple_of((1 - wt) * down_half, 16), down_half), :] = down_recv[...]
    pad = wide - 2 * down_half
    if pad:
        down_w[2 * down_half :, :] = jnp.zeros((pad, down_w.shape[1]), BF)

    def chunk(start, out_ref, out_start):
        rows = pl.ds(start, 2 * tok)
        n2 = n2_all[rows, :]
        gate = kdot(n2, gu_w[:, :wide], 1, 0)
        up = kdot(n2, gu_w[:, wide:], 1, 0)
        grad_act = kdot(cot_all[rows, :], down_w[...], 1, 1)
        sig = jax.nn.sigmoid(gate)
        gated = gate * sig
        act_ref[rows, :] = (gated * up).astype(BF)
        g_gate = (grad_act * up * sig * (1.0 + gate * (1.0 - sig))).astype(BF)
        g_up = (grad_act * gated).astype(BF)
        g_ref[rows, :wide] = g_gate
        g_ref[rows, wide:] = g_up
        grad = kdot(g_gate, gu_w[:, :wide], 1, 1) + kdot(g_up, gu_w[:, wide:], 1, 1)
        out_ref[pl.ds(out_start, 2 * tok), :] = grad.astype(out_ref.dtype)

    for j in range(2):
        chunk(2 * tok * (2 + j), send_ref, 2 * tok * j)
    for j in range(2):
        chunk(2 * tok * j, keep_ref, 2 * tok * j)


def mlp(idx, n2, cot, gu_own, gu_recv, down_own, down_recv):
    tok, dim = n2[0].shape
    wide2 = gu_own.shape[1]
    wide = wide2 // 2
    sds = jax.ShapeDtypeStruct
    return pl.pallas_call(
        mlp_kernel,
        out_shape=(
            sds((4 * tok, dim), F32),
            sds((4 * tok, dim), BF),
            sds((8 * tok, wide2), BF),
            sds((8 * tok, wide), BF),
            sds((8 * tok, dim), BF),
            sds((8 * tok, dim), BF),
            sds((wide, dim), BF),
        ),
        in_specs=[SMEM_SPEC] + [VMEM_SPEC] * 20,
        out_specs=(VMEM_SPEC,) * 7,
        scratch_shapes=[pltpu.VMEM((dim, wide2), BF)],
        compiler_params=pltpu.CompilerParams(vmem_limit_bytes=56 * 2**20),
        name="mlp",
    )(idx, *n2, *cot, gu_own, gu_recv, down_own, down_recv)


def outer_kernel(groups_z, idx_ref, att_ref, gh_ref, n1_ref, gq_ref, mine_ref, send_ref):
    half = gq_ref.shape[1]
    block = mine_ref.shape[1]
    upper = idx_ref[1] == 1
    y_high = idx_ref[0] == 1
    gh = jnp.where(upper, gh_ref[:, half:].astype(F32), gh_ref[:, :half].astype(F32)).astype(BF)
    for part, (left, right) in enumerate(((att_ref[...], gh), (n1_ref[...], gq_ref[...]))):
        full = kdot(left, right, 0, 0)
        cols = slice(part * half, (part + 1) * half)
        for r in range(groups_z):
            low = full[2 * r * block : (2 * r + 1) * block]
            high = full[(2 * r + 1) * block : (2 * r + 2) * block]
            mine_ref[r, :, cols] = jnp.where(y_high, high, low).astype(BF)
            send_ref[r, :, cols] = jnp.where(y_high, low, high).astype(BF)


def outer_terms(idx, att, gh, n1, gq, groups_z):
    dim = att.shape[1]
    shape = jax.ShapeDtypeStruct((groups_z, dim // groups_z // 2, 2 * gq.shape[1]), BF)
    return pl.pallas_call(
        functools.partial(outer_kernel, groups_z),
        out_shape=(shape, shape),
        in_specs=[SMEM_SPEC] + [VMEM_SPEC] * 4,
        out_specs=(VMEM_SPEC, VMEM_SPEC),
        name="outer_terms",
    )(idx, att, gh, n1, gq)


def assemble_kernel(groups_z, ff_blk, ff_wide, factor, idx_ref, parts_ref, gate_ref, up_ref):
    for xyc in range(8):
        plane = (xyc % 4) * 2 + xyc // 4
        part = parts_ref[xyc ^ idx_ref[0]].astype(F32) * factor
        for ref, start in ((gate_ref, 0), (up_ref, ff_wide)):
            for g in range(groups_z):
                col = (g * 8 + plane) * ff_blk
                ref[:, col : col + ff_blk] = part[:, start + g * ff_blk : start + (g + 1) * ff_blk]


def assemble(idx, parts, groups_z, ff_blk, ff_wide, factor):
    rows = parts.shape[1]
    shape = jax.ShapeDtypeStruct((rows, 8 * groups_z * ff_blk), F32)
    return pl.pallas_call(
        functools.partial(assemble_kernel, groups_z, ff_blk, ff_wide, factor),
        out_shape=(shape, shape),
        in_specs=[SMEM_SPEC, VMEM_SPEC],
        out_specs=(VMEM_SPEC, VMEM_SPEC),
        name="assemble",
    )(idx, parts)


def shards(block_input, cotangent, norm_attn, w_qkv, b_qkv, w_out, norm_mlp, w_gate, w_up, w_down):
    ctx_count = lax.axis_size("ctx")
    groups_z = ctx_count // 4
    pairs = ctx_count // 2
    device_count = 2 * ctx_count
    z_bits = groups_z.bit_length() - 1
    _, tok, dim = block_input.shape
    half_tok = tok // 2
    length = tok * ctx_count
    half_dim = dim // 2
    kv_cols = KVH * HD
    ff = w_gate.shape[1]
    ff_blk = ff // device_count
    factor = 1.0 / math.sqrt(2 * length)
    ctx = lax.axis_index("ctx")
    wt = lax.axis_index("wt")
    core = ctx % 2
    chip_y = (ctx // 2) % 2
    pair = ctx // 2
    group = ctx // 4
    plane = (ctx % 4) * 2 + wt

    def swap(a, cx, wx):
        if wx == 0:
            return lax.ppermute(a, "ctx", [(i, i ^ cx) for i in range(ctx_count)])
        if cx == 0:
            return lax.ppermute(a, "wt", [(0, 1), (1, 0)])
        return lax.ppermute(
            a, ("ctx", "wt"), [(i, i ^ (2 * cx + wx)) for i in range(device_count)]
        )

    def shift(a, k):
        return lax.ppermute(a, "ctx", [(i, (i + 4 * k) % ctx_count) for i in range(ctx_count)])

    def by_bit(bit, first, second, axis):
        return jnp.where(
            bit == 0,
            jnp.concatenate([first, second], axis=axis),
            jnp.concatenate([second, first], axis=axis),
        )

    def pick(a, index, axis=0):
        return lax.dynamic_index_in_dim(a, index, axis, keepdims=False)

    def pair_rows(own, peer):
        return jnp.concatenate(
            [own[:half_tok], peer[:half_tok], own[half_tok:], peer[half_tok:]], axis=0
        )

    def own_rows(a):
        return jnp.concatenate([a[:half_tok], a[tok : tok + half_tok]], axis=0)

    def peer_rows(a):
        return jnp.concatenate([a[half_tok:tok], a[tok + half_tok :]], axis=0)

    head_cols = dim // KVH
    rope_cols = head_cols + HD

    def core_cols(a, axis):
        pieces = [
            (head_cols * core, head_cols),
            (dim + HD * core, HD),
            (dim + kv_cols + HD * core, HD),
        ]
        return jnp.concatenate(
            [lax.dynamic_slice_in_dim(a, s, w, axis) for s, w in pieces], axis=axis
        )

    wq_own = core_cols(w_qkv, 1)
    wq_recv = swap(wq_own, 0, 1)
    x_own = block_input[0]
    x_two = pair_rows(x_own, swap(x_own, 1, 0)).astype(F32)
    b_own = core_cols(b_qkv, 0)

    ff_own = groups_z * ff_blk
    ff_pad = -ff_own % 128
    ff_wide = ff_own + ff_pad

    def plane_gather(a):
        four = [a, swap(a, 0, 1), swap(a, 2, 0), swap(a, 2, 1)]
        return four + [swap(v, 1, 0) for v in four]

    def plane_quad(keep, send):
        quad = keep.astype(F32) + swap(send, 1, 0).astype(F32)
        return quad.reshape(4, tok, dim)

    def plane_finish(quad, done=None):
        recv = [
            swap(quad[1].astype(BF), 0, 1),
            swap(quad[2].astype(BF), 2, 0),
            swap(quad[3].astype(BF), 2, 1),
        ]
        if done is not None:
            recv = [after(v, done) for v in recv]
        return quad[0] + recv[0].astype(F32) + recv[1].astype(F32) + recv[2].astype(F32)

    w_out_l, w_gate_l, w_up_l, w_down_l = [after(v, wq_own) for v in (w_out, w_gate, w_up, w_down)]
    wo_recv = swap(lax.dynamic_slice_in_dim(w_out_l, half_dim * core, half_dim, 1), 0, 1)

    def ff_cols(p, gate, up):
        return hidden_columns(p[None].astype(jnp.int32), gate, up, groups_z, ff_blk, ff_wide)

    gu_recv = swap(ff_cols(plane ^ 1, w_gate_l, w_up_l), 0, 1)
    down_shape = (groups_z // 2, 8, ff_blk, dim)
    down_recv = swap(pick(w_down_l.reshape(down_shape), plane ^ 1, 1).reshape(-1, dim), 0, 1)

    normed1, inv1 = rms_norm(x_two, norm_attn)
    normed1_bf = normed1.astype(BF)
    wq = by_bit(wt, wq_own, wq_recv, 0)
    project = dot(normed1_bf, wq) + b_own
    within = jnp.arange(half_tok, dtype=jnp.int32)
    peer = ctx ^ 1
    pos = jnp.concatenate(
        [
            ctx * half_tok + within,
            peer * half_tok + within,
            length - (ctx + 1) * half_tok + within,
            length - (peer + 1) * half_tok + within,
        ]
    )
    steps = jnp.arange(HD // 2, dtype=F32)
    angles = pos.astype(F32)[:, None] * (THETA ** (-2.0 * steps / HD))[None, :]
    cosine = jnp.tile(jnp.cos(angles), (1, 2 * rope_cols // HD))
    sine = jnp.tile(jnp.sin(angles), (1, 2 * rope_cols // HD))

    def halves(u):
        first = (lax.broadcasted_iota(jnp.int32, (1, u.shape[1]), 1) % HD) < HD // 2
        return first, jnp.roll(u, -(HD // 2), axis=1), jnp.roll(u, HD // 2, axis=1)

    def rope(u):
        first, ahead, behind = halves(u)
        return u * cosine + jnp.where(first, -ahead, behind) * sine

    def unrope(g):
        cols = g.shape[1]
        first, ahead, behind = halves(g * sine[:, :cols])
        return g * cosine[:, :cols] + jnp.where(first, ahead, -behind)

    rotated = rope(project[:, :rope_cols]).astype(BF)
    q_scaled = rotated[:, :head_cols] * BF(1.0 / math.sqrt(HD))
    kv_own = jnp.concatenate([rotated[:, head_cols:], project[:, rope_cols:].astype(BF)], axis=1)
    kvs = [kv_own] + [swap(kv_own, 2 * k, 0) for k in range(1, pairs)]

    w_down_l, cot_own = after(w_down, kv_own), after(cotangent[0], kv_own)
    down_own = pick(w_down_l.reshape(down_shape), plane, 1).reshape(-1, dim)
    cot_all = plane_gather(cot_own)

    idx = jnp.stack([pair, core]).astype(jnp.int32)
    att_heads, lse = attention_fwd(idx, q_scaled, kvs)
    att_peer = swap(att_heads, 1, 0)
    wo_other = by_bit(core, wo_recv, swap(after(wo_recv, att_heads), 1, 0), 1)
    wo = by_bit(wt, w_out, wo_other, 0)
    att_peer = pair_rows(peer_rows(att_peer), own_rows(att_peer))
    att_two = by_bit(core, att_heads, att_peer, 1)
    hidden1 = x_own.astype(F32) + dot(own_rows(att_two), wo)
    normed2, inv2 = rms_norm(hidden1, norm_mlp)
    n2 = plane_gather(normed2.astype(BF))
    w_gate_l, w_up_l = after(w_gate, normed2), after(w_up, normed2)
    gu_own = ff_cols(plane, w_gate_l, w_up_l)

    keep, send, g_gu, active, n2_all, cot_all, down_w = mlp(
        wt[None].astype(jnp.int32), n2, cot_all, gu_own, gu_recv, down_own, down_recv
    )
    gn2_quad = plane_quad(keep, send)
    gw_gu = dot(n2_all, g_gu, 0, 0, BF)
    gw_down = dot(active, cot_all, 0, 0, BF)
    out_part = dot(active, down_w, 1, 0, BF)

    def z_half_send(a, bit):
        a = a.reshape((a.shape[0] // 2, 2) + a.shape[1:])
        mine_bit = (group >> bit) & 1
        send = pick(a, 1 - mine_bit, 1)
        mask = 4 << bit
        recv = lax.ppermute(send, "ctx", [(i, i ^ mask) for i in range(ctx_count)])
        return pick(a, mine_bit, 1), recv

    def z_half_add(pair_of):
        return pair_of[0].astype(F32) + pair_of[1].astype(F32)

    def z_half_finish(pair_of, first, last):
        for bit in range(1, z_bits):
            part = z_half_add((pair_of[0], after(pair_of[1], first))).astype(BF)
            pair_of = z_half_send(part, bit)
        return z_half_add((pair_of[0], after(pair_of[1], last)))[0]

    def z_send(a):
        return [pick(a, group)] + [
            shift(pick(a, (group + k) % groups_z), k) for k in range(1, groups_z)
        ]

    def z_add(parts, done):
        total = parts[0].astype(F32)
        for v in parts[1:]:
            total = total + after(v, done).astype(F32)
        return total

    grad_norm2 = plane_finish(gn2_quad)
    gw_gu, gw_down = after(gw_gu, gn2_quad), after(gw_down, gn2_quad)
    z_gu = z_half_send(gw_gu.reshape(groups_z, dim // groups_z, -1), 0)
    z_down = z_half_send(gw_down[:ff_own].reshape(groups_z, ff_blk, dim), 0)

    gg_mlp = jnp.sum(grad_norm2 * hidden1 * inv2, axis=0)
    grad_hidden = cot_own.astype(F32) + norm_back(grad_norm2, hidden1, inv2, norm_mlp)
    gh_own = grad_hidden.astype(BF)
    gh_two = pair_rows(gh_own, swap(gh_own, 1, 0))
    wo_rows = lax.dynamic_slice_in_dim(wo, half_dim * core, half_dim, 0)
    grad_att = dot(gh_two, wo_rows, 1, 1, BF)

    rope_t = jnp.stack([jnp.cos(angles).T, jnp.sin(angles).T])
    gq_bf, gq_sum, dkvs = attention_bwd(idx, q_scaled, grad_att, att_heads, lse, rope_t, kvs)
    dkv_recv = [dkvs[0]] + [swap(dkvs[k], 2 * k, 0) for k in range(1, pairs)]

    yc = jnp.stack([chip_y, core]).astype(jnp.int32)
    oq_mine, oq_send = outer_terms(yc, att_two, gh_two, normed1_bf, gq_bf, groups_z)
    gn1_q = dot(gq_bf, wq[:, :head_cols], 1, 1)
    out_late = after(out_part, oq_send)
    out_quad = plane_quad(out_late[: 4 * tok], out_late[4 * tok :])

    rows = dim // device_count

    def plane_step(a, bit, cx, wx):
        return pick(a, bit), swap(pick(a, 1 - bit), cx, wx)

    oq_recv = swap(oq_send, 2, 0)

    def oq_finish(recv):
        a = (oq_mine.astype(F32) + recv.astype(F32)).astype(BF)
        a = jnp.moveaxis(a.reshape(groups_z, 2, 2 * rows, 2 * head_cols), 1, 0)
        mine, other = plane_step(a, core, 1, 0)
        a = by_bit(core, mine, other, -1)
        a = jnp.moveaxis(a.reshape(groups_z, 2, rows, 4 * head_cols), 1, 0)
        mine, other = plane_step(a, wt, 0, 1)
        return (mine.astype(F32) + other.astype(F32)).astype(BF)

    dkv = dkv_recv[0].astype(F32)
    for v in dkv_recv[1:]:
        dkv = dkv + v.astype(F32)
    gkv = jnp.concatenate([unrope(dkv[:, :HD]), dkv[:, HD:]], axis=1)
    gkv_bf = gkv.astype(BF)
    gn1_part = gn1_q + dot(gkv_bf, wq[:, head_cols:], 1, 1)
    gn1_swap = swap(peer_rows(gn1_part), 1, 0)
    gw_kv = dot(normed1_bf, gkv_bf, 0, 0, BF)
    gb = jnp.concatenate([gq_sum[0], jnp.sum(gkv, axis=0)])
    grad_norm1 = own_rows(gn1_part) + gn1_swap
    x32 = x_own.astype(F32)
    inv1_own = own_rows(inv1)
    gg_attn = jnp.sum(grad_norm1 * x32 * inv1_own, axis=0)

    zero_q = jnp.zeros((head_cols,), F32)
    zero_h = jnp.zeros((HD,), F32)
    gb_full = jnp.concatenate(
        [
            by_bit(core, gb[:head_cols], zero_q, 0),
            by_bit(core, gb[head_cols:rope_cols], zero_h, 0),
            by_bit(core, gb[rope_cols:], zero_h, 0),
        ]
    )
    split_at = dim + kv_cols
    n_qk = split_at // device_count
    n_v = kv_cols // device_count
    small = jnp.concatenate(
        [
            gg_attn.reshape(device_count, rows),
            gg_mlp.reshape(device_count, rows),
            gb_full[:split_at].reshape(device_count, n_qk),
            gb_full[split_at:].reshape(device_count, n_v),
        ],
        axis=1,
    )
    n_small = small.shape[1]
    small = jnp.pad(small, ((0, 0), (0, 2 * HD - n_small)))
    tail = jnp.concatenate(
        [gw_kv.reshape(device_count, rows, 2 * HD), small.astype(BF)[:, None, :]], axis=1
    )
    tail_src = tail
    oq = oq_finish(after(oq_recv, tail_src))
    tail = lax.all_to_all(tail, ("ctx", "wt"), 0, 0, tiled=True)
    tail = tail.reshape(ctx_count // 2, 2, 2, rows + 1, 2 * HD).astype(F32)
    tail = jnp.sum(tail, axis=(0, 2)) * factor

    grad_input = grad_hidden + norm_back(grad_norm1, x32, inv1_own, norm_attn)
    output = (hidden1 + plane_finish(out_quad, tail_src)).astype(BF)
    sum_oq = z_add(z_send(oq), tail_src) * factor
    shard_down = z_half_finish(z_down, oq_send, tail_src) * factor
    sum_gu = z_half_finish(z_gu, oq_send, tail_src).astype(BF)

    a = sum_gu.reshape(2, 2, 2, rows, 2 * ff_wide)
    mine, other = plane_step(jnp.moveaxis(a, 1, 0), core, 1, 0)
    a = jnp.stack([mine, other])
    mine, other = plane_step(jnp.moveaxis(a, 1, 0), chip_y, 2, 0)
    a = jnp.stack([mine, other])
    mine, other = plane_step(jnp.moveaxis(a, 2, 0), wt, 0, 1)
    parts = jnp.stack([mine, other]).reshape(8, rows, 2 * ff_wide)
    here = (wt * 4 + chip_y * 2 + core).astype(jnp.int32)
    shard_gate, shard_up = assemble(here[None], parts, groups_z, ff_blk, ff_wide, factor)

    oq_cols = 2 * head_cols
    shard_wout = jnp.concatenate([sum_oq[:, :head_cols], sum_oq[:, oq_cols:oq_cols + head_cols]], axis=1)
    low, high = tail[0], tail[1]
    shard_qkv = jnp.concatenate(
        [
            sum_oq[:, head_cols:oq_cols],
            sum_oq[:, oq_cols + head_cols :],
            low[:rows, :HD],
            high[:rows, :HD],
            low[:rows, HD:],
            high[:rows, HD:],
        ],
        axis=1,
    )
    vec = low[rows, :n_small] + high[rows, :n_small]
    return (
        output[None],
        grad_input[None],
        vec[:rows],
        shard_qkv,
        vec[2 * rows : 2 * rows + n_qk],
        vec[2 * rows + n_qk :],
        shard_wout,
        vec[rows : 2 * rows],
        shard_gate,
        shard_up,
        shard_down,
    )


def solution(mesh):
    both = P(("ctx", "wt"))
    both_rows = P(("ctx", "wt"), None)
    tokens = P("wt", "ctx", None)
    weight = P("wt", None)
    return jax.shard_map(
        shards,
        mesh=mesh,
        in_specs=(tokens, tokens, P(), weight, P(), weight, P(), weight, weight, weight),
        out_specs=(
            tokens,
            tokens,
            both,
            both_rows,
            both,
            both,
            both_rows,
            both,
            both_rows,
            both_rows,
            both_rows,
        ),
        check_vma=False,
    )
```

```python
import functools
import math

import jax
import jax.numpy as jnp
from jax import lax
from jax.experimental import pallas as pl
from jax.experimental.pallas import tpu as pltpu
from jax.sharding import Mesh
from jax.sharding import PartitionSpec as P

KVH = 2
HD = 64
EPSILON = 1e-06
THETA = 1000000.0
F32 = jnp.float32
BF = jnp.bfloat16
CTX = ("group", "chip", "core")


def rms_norm(hidden, gain):
    inverse = lax.rsqrt(jnp.mean(hidden * hidden, axis=-1, keepdims=True) + EPSILON)
    return (hidden * inverse * gain, inverse)


def norm_back(grad_normed, hidden, inverse, gain):
    scaled = grad_normed * gain
    return inverse * (
        scaled - hidden * inverse * inverse * jnp.mean(scaled * hidden, axis=-1, keepdims=True)
    )


def after(value, done):
    return lax.optimization_barrier((value, done))[0]


def gate_kernel(value_ref, done_ref, out_ref):
    pass


def gate(value, done):
    any_spec = pl.BlockSpec(memory_space=pl.ANY)
    return pl.pallas_call(
        gate_kernel,
        out_shape=jax.ShapeDtypeStruct(value.shape, value.dtype),
        in_specs=[any_spec, any_spec],
        out_specs=any_spec,
        input_output_aliases={0: 0},
        name="gate",
    )(value, done)


def dot(a, b, ca=1, cb=0, out=F32):
    return lax.dot_general(a, b, (((ca,), (cb,)), ((), ())), preferred_element_type=out)


def kdot(a, b, ca, cb, precision=None):
    return lax.dot_general(
        a, b, (((ca,), (cb,)), ((), ())), preferred_element_type=F32, precision=precision
    )


def head_rows(ref, sel, head, blk):
    return ref[sel * blk : (sel + 1) * blk, head * HD : (head + 1) * HD]


def diag_mask(blk, groups, flip):
    shape = (blk, groups * blk)
    key = lax.broadcasted_iota(jnp.int32, shape, 0)
    query = lax.broadcasted_iota(jnp.int32, shape, 1) % blk
    half = blk // 2
    key = jnp.where(flip, (key + half) % blk, key)
    query = jnp.where(flip, (query + half) % blk, query)
    return key <= query


def fwd_kernel(pairs, groups, blk, idx_ref, q_ref, *refs):
    kv_refs = refs[:pairs]
    att_ref, lse_ref, kv_all, qp, scores, acc = refs[pairs:]
    here = idx_ref[0]
    core = idx_ref[1]
    width = groups * blk
    for k in range(pairs):
        kv_all[k] = kv_refs[k][...]
    zeros = jnp.zeros((blk, HD), BF)
    for sel in range(2):
        for head in range(groups):
            qp[sel, head * blk : (head + 1) * blk, :] = jnp.concatenate(
                [head_rows(q_ref, sel, head, blk), zeros], axis=1
            )

    def kv_block(low_high, j):
        return kv_all[j ^ here, pl.ds(pl.multiple_of(low_high * blk, blk), blk), :]

    def fold(top, s):
        return jnp.maximum(top, jnp.max(s.reshape(blk // 8, 8, width), axis=0))

    start = jnp.full((8, width), -1e30, F32)

    def full_step(j, top):
        s = kdot(kv_block(0, j), qp[1], 1, 1)
        scores[j] = s
        return fold(top, s)

    top_high = lax.fori_loop(0, pairs, full_step, start)

    def off_step(u, tops):
        low = u < here
        j = jnp.where(low, u, u + 1)
        sel = jnp.where(low, 0, 1)
        s = kdot(kv_block(sel, j), qp[sel], 1, 1)
        scores[pairs + u] = s
        m = jnp.max(s.reshape(blk // 8, 8, width), axis=0)
        return (
            jnp.where(low, jnp.maximum(tops[0], m), tops[0]),
            jnp.where(low, tops[1], jnp.maximum(tops[1], m)),
        )

    tops = lax.fori_loop(0, pairs - 1, off_step, (start, top_high))
    tops = list(tops)
    for sel in range(2):
        mask = diag_mask(blk, groups, (core == 1) if sel == 0 else (core == 0))
        s = jnp.where(mask, kdot(kv_block(sel, here), qp[sel], 1, 1), -1e30)
        scores[2 * pairs - 1 + sel] = s
        tops[sel] = jnp.max(fold(tops[sel], s), axis=0, keepdims=True)

    def probs(s, top):
        p = jnp.exp(s - top)
        return p.astype(BF), jnp.sum(p.reshape(blk // 8, 8, width), axis=0)

    totals = []
    for sel in range(2):
        pb, t = probs(scores[2 * pairs - 1 + sel], tops[sel])
        acc[sel] = kdot(kv_block(sel, here), pb, 0, 0)
        totals.append(t)

    def full_mix(j, total):
        pb, t = probs(scores[j], tops[1])
        acc[1] += kdot(kv_block(0, j), pb, 0, 0)
        return total + t

    totals[1] = lax.fori_loop(0, pairs, full_mix, totals[1])

    def off_mix(u, totals):
        low = u < here
        j = jnp.where(low, u, u + 1)
        sel = jnp.where(low, 0, 1)
        pb, t = probs(scores[pairs + u], jnp.where(low, tops[0], tops[1]))
        acc[sel] += kdot(kv_block(sel, j), pb, 0, 0)
        return (
            jnp.where(low, totals[0] + t, totals[0]),
            jnp.where(low, totals[1], totals[1] + t),
        )

    totals = lax.fori_loop(0, pairs - 1, off_mix, tuple(totals))
    for sel in range(2):
        total = jnp.sum(totals[sel], axis=0, keepdims=True)
        lse_ref[sel] = tops[sel] + jnp.log(total)
        mixed = acc[sel, HD:, :] / total
        for head in range(groups):
            att_ref[sel * blk : (sel + 1) * blk, head * HD : (head + 1) * HD] = (
                mixed[:, head * blk : (head + 1) * blk].T.astype(BF)
            )


def bwd_kernel(
    pairs, groups, blk, scale, idx_ref, q_ref, do_ref, att_ref, lse_ref, rope_ref, *refs
):
    kv_refs = refs[:pairs]
    gq_ref, gsum_ref = refs[pairs : pairs + 2]
    dkv_refs = refs[pairs + 2 : 2 * pairs + 2]
    kv_all, qp, dop, dkv, dq_acc = refs[2 * pairs + 2 :]
    here = idx_ref[0]
    core = idx_ref[1]
    for k in range(pairs):
        kv_all[k] = kv_refs[k][...]
    zeros = jnp.zeros((blk, HD), BF)
    for sel in range(2):
        for head in range(groups):
            rows = slice(head * blk, (head + 1) * blk)
            qp[sel, rows, :] = jnp.concatenate([head_rows(q_ref, sel, head, blk), zeros], axis=1)
            dop[sel, rows, :] = jnp.concatenate([zeros, head_rows(do_ref, sel, head, blk)], axis=1)
    prod = do_ref[...].astype(F32) * att_ref[...].astype(F32)
    picks_shape = (8, groups * HD)
    picks = (
        lax.broadcasted_iota(jnp.int32, picks_shape, 1) // HD
        == lax.broadcasted_iota(jnp.int32, picks_shape, 0)
    ).astype(F32)
    delta_heads = kdot(picks, prod, 1, 1, lax.Precision.HIGHEST)
    deltas = [
        jnp.concatenate(
            [delta_heads[h : h + 1, sel * blk : (sel + 1) * blk] for h in range(groups)], axis=1
        )
        for sel in range(2)
    ]
    lses = [lse_ref[0], lse_ref[1]]

    def kv_block(low_high, j):
        return kv_all[j ^ here, pl.ds(pl.multiple_of(low_high * blk, blk), blk), :]

    def terms(kv, sel, lse, delta, mask=None):
        s = kdot(kv, qp[sel], 1, 1)
        p = jnp.exp(s - lse) if mask is None else jnp.where(
            mask, jnp.exp(jnp.where(mask, s, -1e30) - lse), 0.0
        )
        dp = kdot(kv, dop[sel], 1, 1)
        ds = (p * (dp - delta)).astype(BF)
        pb = p.astype(BF)
        dk = kdot(ds, qp[sel], 1, 0) + kdot(pb, dop[sel], 1, 0)
        return ds, dk

    for sel in range(2):
        mask = diag_mask(blk, groups, (core == 1) if sel == 0 else (core == 0))
        kv = kv_block(sel, here)
        ds, dk = terms(kv, sel, lses[sel], deltas[sel], mask)
        dq_acc[sel] = kdot(kv, ds, 0, 0)
        dkv[here, sel] = dk

    def full_step(j, carry):
        kv = kv_block(0, j)
        ds, dk = terms(kv, 1, lses[1], deltas[1])
        dq_acc[1] += kdot(kv, ds, 0, 0)

        @pl.when(j == here)
        def _():
            dkv[j, 0] += dk

        @pl.when(j != here)
        def _():
            dkv[j, 0] = dk

        return carry

    lax.fori_loop(0, pairs, full_step, 0)

    def off_step(u, carry):
        low = u < here
        j = jnp.where(low, u, u + 1)
        sel = jnp.where(low, 0, 1)
        kv = kv_block(sel, j)
        ds, dk = terms(
            kv, sel, jnp.where(low, lses[0], lses[1]), jnp.where(low, deltas[0], deltas[1])
        )
        dq_acc[sel] += kdot(kv, ds, 0, 0)

        @pl.when(low)
        def _():
            dkv[j, 0] += dk
            dkv[j, 1] = jnp.zeros_like(dk)

        @pl.when(jnp.logical_not(low))
        def _():
            dkv[j, 1] = dk

        return carry

    lax.fori_loop(0, pairs - 1, off_step, 0)
    for k in range(pairs):
        for sel in range(2):
            dkv_refs[k][sel * blk : (sel + 1) * blk, :] = dkv[k ^ here, sel].astype(
                dkv_refs[k].dtype
            )
    for head in range(groups):
        cols = slice(head * HD, (head + 1) * HD)
        total = jnp.zeros((1, HD), F32)
        for sel in range(2):
            rows = slice(sel * blk, (sel + 1) * blk)
            cosine = rope_ref[0, :, rows]
            sine = rope_ref[1, :, rows]
            turned = dq_acc[sel, :HD, head * blk : (head + 1) * blk] * scale
            low, high = turned[: HD // 2], turned[HD // 2 :]
            back = jnp.concatenate(
                [low * cosine + high * sine, high * cosine - low * sine], axis=0
            ).T
            gq_ref[rows, cols] = back.astype(BF)
            total = total + jnp.sum(back, axis=0, keepdims=True)
        gsum_ref[:, cols] = total


VMEM_SPEC = pl.BlockSpec(memory_space=pltpu.VMEM)
SMEM_SPEC = pl.BlockSpec(memory_space=pltpu.SMEM)


def attention_fwd(idx, q, kvs):
    pairs = len(kvs)
    rows, cols = q.shape
    blk = rows // 2
    groups = cols // HD
    width = groups * blk
    return pl.pallas_call(
        functools.partial(fwd_kernel, pairs, groups, blk),
        out_shape=(
            jax.ShapeDtypeStruct((rows, cols), BF),
            jax.ShapeDtypeStruct((2, 1, width), F32),
        ),
        in_specs=[SMEM_SPEC] + [VMEM_SPEC] * (1 + pairs),
        out_specs=(VMEM_SPEC, VMEM_SPEC),
        scratch_shapes=[
            pltpu.VMEM((pairs, rows, 2 * HD), BF),
            pltpu.VMEM((2, width, 2 * HD), BF),
            pltpu.VMEM((2 * pairs + 1, blk, width), F32),
            pltpu.VMEM((2, 2 * HD, width), F32),
        ],
        compiler_params=pltpu.CompilerParams(vmem_limit_bytes=56 * 2**20),
        name="attn_fwd",
    )(idx, q, *kvs)


def attention_bwd(idx, q, d_out, att, lse, rope_t, kvs):
    pairs = len(kvs)
    rows, cols = q.shape
    blk = rows // 2
    groups = cols // HD
    width = groups * blk
    res = pl.pallas_call(
        functools.partial(bwd_kernel, pairs, groups, blk, 1.0 / math.sqrt(HD)),
        out_shape=(jax.ShapeDtypeStruct((rows, cols), BF), jax.ShapeDtypeStruct((1, cols), F32))
        + tuple(jax.ShapeDtypeStruct((rows, 2 * HD), BF) for _ in range(pairs)),
        in_specs=[SMEM_SPEC] + [VMEM_SPEC] * (5 + pairs),
        out_specs=(VMEM_SPEC,) * (2 + pairs),
        scratch_shapes=[
            pltpu.VMEM((pairs, rows, 2 * HD), BF),
            pltpu.VMEM((2, width, 2 * HD), BF),
            pltpu.VMEM((2, width, 2 * HD), BF),
            pltpu.VMEM((pairs, 2, blk, 2 * HD), F32),
            pltpu.VMEM((2, 2 * HD, width), F32),
        ],
        compiler_params=pltpu.CompilerParams(vmem_limit_bytes=56 * 2**20),
        name="attn_bwd",
    )(idx, q, d_out, att, lse, rope_t, *kvs)
    return res[0], res[1], res[2:]


def columns_kernel(groups_z, ff_blk, ff_wide, window, rows, idx_ref, gate_ref, up_ref, out_ref, win, sems):
    ff = gate_ref.shape[1]
    here = idx_ref[0]
    shifts = []
    copies = []
    for m, ref in enumerate((gate_ref, up_ref)):
        for g in range(groups_z):
            col = (g * 8 + here) * ff_blk
            start = jnp.minimum((col // 128) * 128, ff - window)
            if m == 0:
                shifts.append(col - start)
            copies.append(
                pltpu.make_async_copy(
                    ref.at[
                        pl.ds(pl.multiple_of(idx_ref[1] * rows, 16), rows),
                        pl.ds(pl.multiple_of(start, 128), window),
                    ],
                    win.at[m * groups_z + g],
                    sems.at[m * groups_z + g],
                )
            )
    for copy in copies:
        copy.start()
    for m in range(2):
        pieces = [None] * (ff_wide // 128)
        for g in range(groups_z):
            first = g * ff_blk // 128
            lead = g * ff_blk - first * 128
            tiles = -(-(lead + ff_blk) // 128)
            copies[m * groups_z + g].wait()
            row = lax.broadcasted_iota(jnp.int32, (window, tiles * 128), 0)
            lane = lax.broadcasted_iota(jnp.int32, (window, tiles * 128), 1) - lead
            hot = jnp.logical_and(row == lane + shifts[g], jnp.logical_and(lane >= 0, lane < ff_blk))
            part = kdot(win[m * groups_z + g], hot.astype(F32).astype(BF), 1, 0)
            for t in range(tiles):
                tile = part[:, t * 128 : (t + 1) * 128]
                old = pieces[first + t]
                pieces[first + t] = tile if old is None else old + tile
        for t, tile in enumerate(pieces):
            col = m * ff_wide + t * 128
            out_ref[:, col : col + 128] = (
                jnp.zeros((out_ref.shape[0], 128), BF) if tile is None else tile.astype(BF)
            )


def hidden_columns(idx, gate, up, groups_z, ff_blk, ff_wide, rows):
    ff = gate.shape[1]
    window = min(-(-(ff_blk + 127) // 128) * 128, ff)
    return pl.pallas_call(
        functools.partial(columns_kernel, groups_z, ff_blk, ff_wide, window, rows),
        out_shape=jax.ShapeDtypeStruct((rows, 2 * ff_wide), BF),
        in_specs=[SMEM_SPEC, pl.BlockSpec(memory_space=pl.ANY), pl.BlockSpec(memory_space=pl.ANY)],
        out_specs=VMEM_SPEC,
        scratch_shapes=[
            pltpu.VMEM((2 * groups_z, rows, window), BF),
            pltpu.SemaphoreType.DMA((2 * groups_z,)),
        ],
        name="hidden_columns",
    )(idx, gate, up)


def mlp_kernel(idx_ref, *refs):
    n2_refs, cot_refs = refs[:8], refs[8:16]
    gu_refs, down_refs = refs[16:19], refs[19:22]
    keep_ref, send_ref, g_ref, act_ref, n2_all, cot_all, down_w = refs[22:29]
    gu_w = refs[29]
    wt = idx_ref[0]
    odd = idx_ref[1]
    tok = n2_refs[0].shape[0]
    wide = gu_w.shape[1] // 2
    down_half = down_refs[0].shape[0]
    for k in range(8):
        n2_all[k * tok : (k + 1) * tok, :] = n2_refs[k][...]
        cot_all[k * tok : (k + 1) * tok, :] = cot_refs[k][...]
    for full, (own, first, second) in ((gu_w, gu_refs), (down_w, down_refs)):
        half, quarter = own.shape[0], first.shape[0]
        for w in range(2):

            @pl.when(wt == w)
            def _():
                full[w * half : (w + 1) * half, :] = own[...]

            other = (1 - w) * half
            for z in range(2):

                @pl.when(jnp.logical_and(wt == w, odd == z))
                def _():
                    at = other + z * quarter
                    full[at : at + quarter, :] = first[...]
                    at = other + (1 - z) * quarter
                    full[at : at + quarter, :] = second[...]

    pad = wide - 2 * down_half
    if pad:
        down_w[2 * down_half :, :] = jnp.zeros((pad, down_w.shape[1]), BF)

    def chunk(start, out_ref, out_start):
        rows = pl.ds(start, 2 * tok)
        n2 = n2_all[rows, :]
        gate = kdot(n2, gu_w[:, :wide], 1, 0)
        up = kdot(n2, gu_w[:, wide:], 1, 0)
        grad_act = kdot(cot_all[rows, :], down_w[...], 1, 1)
        sig = jax.nn.sigmoid(gate)
        gated = gate * sig
        act_ref[rows, :] = (gated * up).astype(BF)
        g_gate = (grad_act * up * sig * (1.0 + gate * (1.0 - sig))).astype(BF)
        g_up = (grad_act * gated).astype(BF)
        g_ref[rows, :wide] = g_gate
        g_ref[rows, wide:] = g_up
        grad = kdot(g_gate, gu_w[:, :wide], 1, 1) + kdot(g_up, gu_w[:, wide:], 1, 1)
        out_ref[pl.ds(out_start, 2 * tok), :] = grad.astype(out_ref.dtype)

    for j in range(2):
        chunk(2 * tok * (2 + j), send_ref, 2 * tok * j)
    for j in range(2):
        chunk(2 * tok * j, keep_ref, 2 * tok * j)


def mlp(idx, n2, cot, gu, down):
    tok, dim = n2[0].shape
    wide2 = gu[0].shape[1]
    wide = wide2 // 2
    sds = jax.ShapeDtypeStruct
    return pl.pallas_call(
        mlp_kernel,
        out_shape=(
            sds((4 * tok, dim), F32),
            sds((4 * tok, dim), BF),
            sds((8 * tok, wide2), BF),
            sds((8 * tok, wide), BF),
            sds((8 * tok, dim), BF),
            sds((8 * tok, dim), BF),
            sds((wide, dim), BF),
        ),
        in_specs=[SMEM_SPEC] + [VMEM_SPEC] * 22,
        out_specs=(VMEM_SPEC,) * 7,
        scratch_shapes=[pltpu.VMEM((dim, wide2), BF)],
        compiler_params=pltpu.CompilerParams(vmem_limit_bytes=56 * 2**20),
        name="mlp",
    )(idx, *n2, *cot, *gu, *down)


def outer_kernel(blocks, idx_ref, att_ref, gh_ref, n1_ref, gq_ref, mine_ref, send_ref):
    half = gq_ref.shape[1]
    rows = mine_ref.shape[1] // 2
    upper = idx_ref[1] == 1
    second = idx_ref[0] == 1
    gh = jnp.where(upper, gh_ref[:, half:].astype(F32), gh_ref[:, :half].astype(F32)).astype(BF)
    for part, (left, right) in enumerate(((att_ref[...], gh), (n1_ref[...], gq_ref[...]))):
        full = kdot(left, right, 0, 0)
        cols = slice(part * half, (part + 1) * half)
        for b in range(blocks):
            low = full[2 * b * rows : (2 * b + 1) * rows]
            high = full[(2 * b + 1) * rows : (2 * b + 2) * rows]
            at = slice(b % 2 * rows, (b % 2 + 1) * rows)
            mine_ref[b // 2, at, cols] = jnp.where(second, high, low).astype(BF)
            send_ref[b // 2, at, cols] = jnp.where(second, low, high).astype(BF)


def outer_terms(idx, att, gh, n1, gq, blocks):
    dim = att.shape[1]
    shape = jax.ShapeDtypeStruct((blocks // 2, dim // blocks, 2 * gq.shape[1]), BF)
    return pl.pallas_call(
        functools.partial(outer_kernel, blocks),
        out_shape=(shape, shape),
        in_specs=[SMEM_SPEC] + [VMEM_SPEC] * 4,
        out_specs=(VMEM_SPEC, VMEM_SPEC),
        name="outer_terms",
    )(idx, att, gh, n1, gq)


def assemble_kernel(groups_z, ff_blk, ff_wide, factor, idx_ref, *refs):
    part_refs = refs[:8]
    gate_ref, up_ref, parts = refs[8:]
    for k in range(8):
        parts[k] = part_refs[k][...].astype(F32) * factor
    for plane in range(8):
        part = parts[plane ^ idx_ref[0]]
        for ref, start in ((gate_ref, 0), (up_ref, ff_wide)):
            for g in range(groups_z):
                col = (g * 8 + plane) * ff_blk
                ref[:, col : col + ff_blk] = part[:, start + g * ff_blk : start + (g + 1) * ff_blk]


def assemble(idx, parts, groups_z, ff_blk, ff_wide, factor):
    rows = parts[0].shape[0]
    shape = jax.ShapeDtypeStruct((rows, 8 * groups_z * ff_blk), F32)
    return pl.pallas_call(
        functools.partial(assemble_kernel, groups_z, ff_blk, ff_wide, factor),
        out_shape=(shape, shape),
        in_specs=[SMEM_SPEC] + [VMEM_SPEC] * 8,
        out_specs=(VMEM_SPEC, VMEM_SPEC),
        scratch_shapes=[pltpu.VMEM((8, rows, 2 * ff_wide), F32)],
        name="assemble",
    )(idx, *parts)


def shards(block_input, cotangent, norm_attn, w_qkv, b_qkv, w_out, norm_mlp, w_gate, w_up, w_down):
    ctx_count = lax.axis_size(CTX)
    groups_z = ctx_count // 4
    pairs = ctx_count // 2
    device_count = 2 * ctx_count
    z_bits = groups_z.bit_length() - 1
    _, tok, dim = block_input.shape
    half_tok = tok // 2
    length = tok * ctx_count
    half_dim = dim // 2
    kv_cols = KVH * HD
    ff = w_gate.shape[1]
    ff_blk = ff // device_count
    factor = 1.0 / math.sqrt(2 * length)
    ctx = lax.axis_index(CTX)
    wt = lax.axis_index("wt")
    core = ctx % 2
    chip_y = (ctx // 2) % 2
    pair = ctx // 2
    group = ctx // 4
    plane = (ctx % 4) * 2 + wt

    def swap_of(a, cx, wx):
        if wx == 0:
            return lax.ppermute(a, CTX, [(i, i ^ cx) for i in range(ctx_count)])
        if cx == 0:
            return lax.ppermute(a, "wt", [(0, 1), (1, 0)])
        return lax.ppermute(
            a, CTX + ("wt",), [(i, i ^ (2 * cx + wx)) for i in range(device_count)]
        )

    def by_bit(bit, first, second, axis):
        return jnp.where(
            bit == 0,
            jnp.concatenate([first, second], axis=axis),
            jnp.concatenate([second, first], axis=axis),
        )

    def pick(a, index, axis=0):
        return lax.dynamic_index_in_dim(a, index, axis, keepdims=False)

    def pair_rows(own, peer):
        return jnp.concatenate(
            [own[:half_tok], peer[:half_tok], own[half_tok:], peer[half_tok:]], axis=0
        )

    def own_rows(a):
        return jnp.concatenate([a[:half_tok], a[tok : tok + half_tok]], axis=0)

    def peer_rows(a):
        return jnp.concatenate([a[half_tok:tok], a[tok + half_tok :]], axis=0)

    head_cols = dim // KVH
    rope_cols = head_cols + HD

    def core_cols(a, axis):
        pieces = [
            (head_cols * core, head_cols),
            (dim + HD * core, HD),
            (dim + kv_cols + HD * core, HD),
        ]
        return jnp.concatenate(
            [lax.dynamic_slice_in_dim(a, s, w, axis) for s, w in pieces], axis=axis
        )

    wq_own = core_cols(w_qkv, 1)
    wq_recv = swap_of(wq_own, 0, 1)
    x_own = block_input[0]
    x_two = pair_rows(x_own, swap_of(x_own, 1, 0)).astype(F32)
    b_own = core_cols(b_qkv, 0)

    ff_own = groups_z * ff_blk
    ff_pad = -ff_own % 128
    ff_wide = ff_own + ff_pad

    def plane_gather(a, filler=None):
        four = [a, swap_of(a, 0, 1), swap_of(a, 2, 0), swap_of(a, 2, 1)]
        if filler is not None:
            four = [a] + [after(v, filler) for v in four[1:]]
        return four + [swap_of(v, 1, 0) for v in four]

    def plane_quad(keep, send):
        quad = keep.astype(F32) + swap_of(send, 1, 0).astype(F32)
        return quad.reshape(4, tok, dim)

    def plane_sends(quad):
        return [
            swap_of(quad[1].astype(BF), 0, 1),
            swap_of(quad[2].astype(BF), 2, 0),
            swap_of(quad[3].astype(BF), 2, 1),
        ]

    def plane_finish(quad, recv):
        return quad[0] + recv[0].astype(F32) + recv[1].astype(F32) + recv[2].astype(F32)

    def ff_cols(p, part, gate, up, rows):
        at = jnp.stack([p, part]).astype(jnp.int32)
        return hidden_columns(at, gate, up, groups_z, ff_blk, ff_wide, rows)

    w_out_l, cot_own = after(w_out, wq_own), after(cotangent[0], wq_own)
    wo_recv = swap_of(lax.dynamic_slice_in_dim(w_out_l, half_dim * core, half_dim, 1), 0, 1)
    cot_all = plane_gather(cot_own)

    z_odd = group & 1

    def z_next_of(a):
        return lax.ppermute(a, CTX, [(i, i ^ 4) for i in range(ctx_count)])

    normed1, inv1 = rms_norm(x_two, norm_attn)
    normed1_bf = normed1.astype(BF)
    wq = by_bit(wt, wq_own, wq_recv, 0)
    project = dot(normed1_bf, wq) + b_own
    within = jnp.arange(half_tok, dtype=jnp.int32)
    peer = ctx ^ 1
    pos = jnp.concatenate(
        [
            ctx * half_tok + within,
            peer * half_tok + within,
            length - (ctx + 1) * half_tok + within,
            length - (peer + 1) * half_tok + within,
        ]
    )
    steps = jnp.arange(HD // 2, dtype=F32)
    angles = pos.astype(F32)[:, None] * (THETA ** (-2.0 * steps / HD))[None, :]
    cosine = jnp.tile(jnp.cos(angles), (1, 2 * rope_cols // HD))
    sine = jnp.tile(jnp.sin(angles), (1, 2 * rope_cols // HD))

    def halves(u):
        first = (lax.broadcasted_iota(jnp.int32, (1, u.shape[1]), 1) % HD) < HD // 2
        return first, jnp.roll(u, -(HD // 2), axis=1), jnp.roll(u, HD // 2, axis=1)

    def rope(u):
        first, ahead, behind = halves(u)
        return u * cosine + jnp.where(first, -ahead, behind) * sine

    def unrope(g):
        cols = g.shape[1]
        first, ahead, behind = halves(g * sine[:, :cols])
        return g * cosine[:, :cols] + jnp.where(first, ahead, -behind)

    rotated = rope(project[:, :rope_cols]).astype(BF)
    q_scaled = rotated[:, :head_cols] * BF(1.0 / math.sqrt(HD))
    kv_own = jnp.concatenate([rotated[:, head_cols:], project[:, rope_cols:].astype(BF)], axis=1)
    kvs = [kv_own] + [swap_of(kv_own, 2 * k, 0) for k in range(1, pairs)]

    w_gate_l, w_up_l = after(w_gate, kv_own), after(w_up, kv_own)
    w_down_l = after(w_down, kv_own)
    down_shape = (groups_z // 2, 8, ff_blk, dim)
    gu_first = swap_of(ff_cols(plane ^ 1, z_odd, w_gate_l, w_up_l, half_dim // 2), 0, 1)
    down_peer = w_down_l.reshape(2, -1, 8, ff_blk, dim)
    down_peer = pick(pick(down_peer, plane ^ 1, 2), z_odd).reshape(-1, dim)
    down_first = swap_of(down_peer, 0, 1)
    gu_second = z_next_of(after(gu_first, kv_own))
    down_second = z_next_of(after(down_first, kv_own))
    down_own = pick(w_down_l.reshape(down_shape), plane, 1).reshape(-1, dim)
    idx = jnp.stack([pair, core]).astype(jnp.int32)
    att_heads, lse = attention_fwd(idx, q_scaled, kvs)
    att_peer = swap_of(att_heads, 1, 0)
    wo_other = by_bit(core, wo_recv, swap_of(after(wo_recv, att_heads), 1, 0), 1)
    wo = by_bit(wt, w_out, wo_other, 0)
    att_peer = pair_rows(peer_rows(att_peer), own_rows(att_peer))
    att_two = by_bit(core, att_heads, att_peer, 1)
    hidden1 = x_own.astype(F32) + dot(own_rows(att_two), wo)
    normed2, inv2 = rms_norm(hidden1, norm_mlp)
    normed2_bf = normed2.astype(BF)
    w_gate_l, w_up_l = after(w_gate, normed2_bf), after(w_up, normed2_bf)
    gu_own = ff_cols(plane, jnp.int32(0), w_gate_l, w_up_l, half_dim)
    n2 = plane_gather(normed2_bf, (gu_own, down_own))

    keep, send, g_gu, active, n2_all, cot_all, down_w = mlp(
        jnp.stack([wt, z_odd]).astype(jnp.int32),
        n2,
        cot_all,
        (gu_own, gu_first, gu_second),
        (down_own, down_first, down_second),
    )
    gn2_quad = plane_quad(keep, send)
    out_keep = dot(active[: 4 * tok], down_w, 1, 0, BF)
    out_send = dot(active[4 * tok :], down_w, 1, 0, BF)
    n2_l, active_l = after(n2_all, gn2_quad), after(active, gn2_quad)
    gw_down = dot(active_l, cot_all, 0, 0, BF)
    gw_gu = dot(n2_l, g_gu, 0, 0, BF)

    def z_half_send(a, bit):
        a = a.reshape((a.shape[0] // 2, 2) + a.shape[1:])
        mine_bit = (group >> bit) & 1
        send = pick(a, 1 - mine_bit, 1)
        mask = 4 << bit
        recv = lax.ppermute(send, CTX, [(i, i ^ mask) for i in range(ctx_count)])
        return pick(a, mine_bit, 1), recv

    def z_half_add(pair_of):
        return pair_of[0].astype(F32) + pair_of[1].astype(F32)

    def z_half_more(pair_of, done):
        for bit in range(1, z_bits):
            part = z_half_add((pair_of[0], after(pair_of[1], done))).astype(BF)
            pair_of = z_half_send(part, bit)
        return pair_of, part

    def z_half_last(pair_of, done):
        return z_half_add((pair_of[0], gate(pair_of[1], done)))[0]

    gn_recv = plane_sends(gn2_quad)
    gn_recv[0] = after(gn_recv[0], (gw_gu, gw_down))
    grad_norm2 = plane_finish(gn2_quad, gn_recv)
    z_gu = z_half_send(gw_gu.reshape(groups_z, dim // groups_z, -1), 0)
    z_down = z_half_send(gw_down[:ff_own].reshape(groups_z, ff_blk, dim), 0)

    gg_mlp = jnp.sum(grad_norm2 * hidden1 * inv2, axis=0)
    grad_hidden = cot_own.astype(F32) + norm_back(grad_norm2, hidden1, inv2, norm_mlp)
    gh_own = grad_hidden.astype(BF)
    gh_two = pair_rows(gh_own, swap_of(gh_own, 1, 0))
    wo_rows = lax.dynamic_slice_in_dim(wo, half_dim * core, half_dim, 0)
    grad_att = dot(gh_two, wo_rows, 1, 1, BF)

    rope_t = jnp.stack([jnp.cos(angles).T, jnp.sin(angles).T])
    gq_bf, gq_sum, dkvs = attention_bwd(idx, q_scaled, grad_att, att_heads, lse, rope_t, kvs)
    dkv_recv = [dkvs[0]] + [swap_of(dkvs[k], 2 * k, 0) for k in range(1, pairs)]

    xc = jnp.stack([wt, core]).astype(jnp.int32)
    oq_mine, oq_send = outer_terms(xc, att_two, gh_two, normed1_bf, gq_bf, ctx_count)
    gn1_q = dot(gq_bf, wq[:, :head_cols], 1, 1)

    rows = dim // device_count

    def plane_step(a, bit, cx, wx):
        return pick(a, bit), swap_of(pick(a, 1 - bit), cx, wx)

    oq_recv = swap_of(oq_send, 0, 1)
    z_down, _ = z_half_more(z_down, gh_own)
    z_gu, _ = z_half_more(z_gu, oq_send)
    out_quad = plane_quad(out_keep, out_send)
    out_recv = plane_sends(out_quad)

    dkv = dkv_recv[0].astype(F32)
    for v in dkv_recv[1:]:
        dkv = dkv + v.astype(F32)
    gkv = jnp.concatenate([unrope(dkv[:, :HD]), dkv[:, HD:]], axis=1)
    gkv_bf = gkv.astype(BF)
    gn1_part = gn1_q + dot(gkv_bf, wq[:, head_cols:], 1, 1)
    gn1_swap = swap_of(peer_rows(gn1_part), 1, 0)
    gw_kv = dot(normed1_bf, gkv_bf, 0, 0, BF)
    gb = jnp.concatenate([gq_sum[0], jnp.sum(gkv, axis=0)])
    grad_norm1 = own_rows(gn1_part) + gn1_swap
    x32 = x_own.astype(F32)
    inv1_own = own_rows(inv1)
    gg_attn = jnp.sum(grad_norm1 * x32 * inv1_own, axis=0)

    zero_q = jnp.zeros((head_cols,), F32)
    zero_h = jnp.zeros((HD,), F32)
    gb_full = jnp.concatenate(
        [
            by_bit(core, gb[:head_cols], zero_q, 0),
            by_bit(core, gb[head_cols:rope_cols], zero_h, 0),
            by_bit(core, gb[rope_cols:], zero_h, 0),
        ]
    )
    split_at = dim + kv_cols
    n_qk = split_at // device_count
    n_v = kv_cols // device_count
    small = jnp.concatenate(
        [
            gg_attn.reshape(device_count, rows),
            gg_mlp.reshape(device_count, rows),
            gb_full[:split_at].reshape(device_count, n_qk),
            gb_full[split_at:].reshape(device_count, n_v),
        ],
        axis=1,
    )
    n_small = small.shape[1]
    small = jnp.pad(small, ((0, 0), (0, 2 * HD - n_small)))
    tail = jnp.concatenate(
        [gw_kv.reshape(device_count, rows, 2 * HD), small.astype(BF)[:, None, :]], axis=1
    )
    tail_src = tail
    tail = tail.reshape(groups_z, 2, 2, 2, rows + 1, 2 * HD)
    tail = jnp.moveaxis(tail, (1, 3), (0, 1))
    kv_mine, kv_recv = plane_step(tail, chip_y, 2, 0)
    oq = (oq_mine.astype(F32) + gate(oq_recv, tail_src).astype(F32)).astype(BF)
    oq = jnp.moveaxis(oq.reshape(groups_z, 2, 2 * rows, 2 * head_cols), 1, 0)
    oq_mine, oq_recv = plane_step(oq, chip_y, 2, 0)
    tail = (kv_mine.astype(F32) + kv_recv.astype(F32)).astype(BF)
    kv_mine, kv_recv = plane_step(tail, wt, 0, 1)
    last = jnp.concatenate(
        [
            jnp.pad(
                (oq_mine.astype(F32) + gate(oq_recv, kv_mine).astype(F32)).reshape(
                    groups_z, 2, rows, 2 * head_cols
                ),
                ((0, 0), (0, 0), (0, 1), (0, 0)),
            ),
            kv_mine.astype(F32) + kv_recv.astype(F32),
        ],
        axis=-1,
    ).astype(BF)
    sum_gu = z_half_last(z_gu, last).astype(BF)
    sum_gu = sum_gu.reshape(8, rows, 2 * ff_wide)
    parts = [pick(sum_gu, plane)] + [
        swap_of(pick(sum_gu, plane ^ k), k >> 1, k & 1) for k in range(1, 8)
    ]
    last = last.reshape(ctx_count // 2, rows + 1, -1)
    last_all = lax.all_to_all(last, ("group", "core"), 0, 0, tiled=True)
    output = (hidden1 + plane_finish(out_quad, [gate(out_recv[0], last)] + out_recv[1:])).astype(BF)
    grad_input = grad_hidden + norm_back(after(grad_norm1, last), x32, inv1_own, norm_attn)
    shard_down = z_half_last(z_down, last) * factor
    last_all = last_all.reshape(groups_z, 2, rows + 1, -1).astype(F32)
    last_sum = jnp.sum(last_all, axis=0) * factor
    sum_oq, tail = last_sum[:, :rows, : 2 * head_cols], last_sum[:, :, 2 * head_cols :]
    shard_gate, shard_up = assemble(plane[None].astype(jnp.int32), parts, groups_z, ff_blk, ff_wide, factor)

    shard_wout = jnp.concatenate([sum_oq[0, :, :head_cols], sum_oq[1, :, :head_cols]], axis=1)
    low, high = tail[0], tail[1]
    shard_qkv = jnp.concatenate(
        [
            sum_oq[0, :, head_cols:],
            sum_oq[1, :, head_cols:],
            low[:rows, :HD],
            high[:rows, :HD],
            low[:rows, HD:],
            high[:rows, HD:],
        ],
        axis=1,
    )
    vec = low[rows, :n_small] + high[rows, :n_small]
    return (
        output[None],
        grad_input[None],
        vec[:rows],
        shard_qkv,
        vec[2 * rows : 2 * rows + n_qk],
        vec[2 * rows + n_qk :],
        shard_wout,
        vec[rows : 2 * rows],
        shard_gate,
        shard_up,
        shard_down,
    )


def solution(mesh):
    ctx_count, wt_count = mesh.devices.shape
    split = Mesh(mesh.devices.reshape(ctx_count // 4, 2, 2, wt_count), CTX + ("wt",))
    both = P(CTX + ("wt",))
    both_rows = P(CTX + ("wt",), None)
    tokens = P("wt", CTX, None)
    weight = P("wt", None)

    return jax.shard_map(
        shards,
        mesh=split,
        in_specs=(tokens, tokens, P(), weight, P(), weight, P(), weight, weight, weight),
        out_specs=(tokens, tokens, both, both_rows, both, both)
        + (both_rows, both, both_rows, both_rows, both_rows),
        check_vma=False,
    )
```

```python
import functools
import math

import jax
import jax.numpy as jnp
from jax import lax
from jax.experimental import pallas as pl
from jax.experimental.pallas import tpu as pltpu
from jax.sharding import Mesh
from jax.sharding import PartitionSpec as P

KVH = 2
HD = 64
EPSILON = 1e-06
THETA = 1000000.0
F32 = jnp.float32
BF = jnp.bfloat16
CTX = ("group", "chip", "core")


def rms_norm(hidden, gain):
    inverse = lax.rsqrt(jnp.mean(hidden * hidden, axis=-1, keepdims=True) + EPSILON)
    return (hidden * inverse * gain, inverse)


def norm_back(grad_normed, hidden, inverse, gain):
    scaled = grad_normed * gain
    return inverse * (
        scaled - hidden * inverse * inverse * jnp.mean(scaled * hidden, axis=-1, keepdims=True)
    )


def after(value, done):
    return lax.optimization_barrier((value, done))[0]


def gate_kernel(value_ref, done_ref, out_ref):
    pass


def gate(value, done):
    any_spec = pl.BlockSpec(memory_space=pl.ANY)
    return pl.pallas_call(
        gate_kernel,
        out_shape=jax.ShapeDtypeStruct(value.shape, value.dtype),
        in_specs=[any_spec, any_spec],
        out_specs=any_spec,
        input_output_aliases={0: 0},
        name="gate",
    )(value, done)


def dot(a, b, ca=1, cb=0, out=F32):
    return lax.dot_general(a, b, (((ca,), (cb,)), ((), ())), preferred_element_type=out)


def kdot(a, b, ca, cb, precision=None):
    return lax.dot_general(
        a, b, (((ca,), (cb,)), ((), ())), preferred_element_type=F32, precision=precision
    )


def head_rows(ref, sel, head, blk):
    return ref[sel * blk : (sel + 1) * blk, head * HD : (head + 1) * HD]


def diag_mask(blk, groups, flip):
    shape = (blk, groups * blk)
    key = lax.broadcasted_iota(jnp.int32, shape, 0)
    query = lax.broadcasted_iota(jnp.int32, shape, 1) % blk
    half = blk // 2
    key = jnp.where(flip, (key + half) % blk, key)
    query = jnp.where(flip, (query + half) % blk, query)
    return key <= query


def fwd_kernel(pairs, groups, blk, idx_ref, q_ref, *refs):
    kv_refs = refs[:pairs]
    att_ref, lse_ref, kv_all, qp, scores, acc = refs[pairs:]
    here = idx_ref[0]
    core = idx_ref[1]
    width = groups * blk
    for k in range(pairs):
        kv_all[k] = kv_refs[k][...]
    zeros = jnp.zeros((blk, HD), BF)
    for sel in range(2):
        for head in range(groups):
            qp[sel, head * blk : (head + 1) * blk, :] = jnp.concatenate(
                [head_rows(q_ref, sel, head, blk), zeros], axis=1
            )

    def kv_block(low_high, j):
        return kv_all[j ^ here, pl.ds(pl.multiple_of(low_high * blk, blk), blk), :]

    def fold(top, s):
        return jnp.maximum(top, jnp.max(s.reshape(blk // 8, 8, width), axis=0))

    start = jnp.full((8, width), -1e30, F32)

    def full_step(j, top):
        s = kdot(kv_block(0, j), qp[1], 1, 1)
        scores[j] = s
        return fold(top, s)

    top_high = lax.fori_loop(0, pairs, full_step, start)

    def off_step(u, tops):
        low = u < here
        j = jnp.where(low, u, u + 1)
        sel = jnp.where(low, 0, 1)
        s = kdot(kv_block(sel, j), qp[sel], 1, 1)
        scores[pairs + u] = s
        m = jnp.max(s.reshape(blk // 8, 8, width), axis=0)
        return (
            jnp.where(low, jnp.maximum(tops[0], m), tops[0]),
            jnp.where(low, tops[1], jnp.maximum(tops[1], m)),
        )

    tops = lax.fori_loop(0, pairs - 1, off_step, (start, top_high))
    tops = list(tops)
    for sel in range(2):
        mask = diag_mask(blk, groups, (core == 1) if sel == 0 else (core == 0))
        s = jnp.where(mask, kdot(kv_block(sel, here), qp[sel], 1, 1), -1e30)
        scores[2 * pairs - 1 + sel] = s
        tops[sel] = jnp.max(fold(tops[sel], s), axis=0, keepdims=True)

    def probs(s, top):
        p = jnp.exp(s - top)
        return p.astype(BF), jnp.sum(p.reshape(blk // 8, 8, width), axis=0)

    totals = []
    for sel in range(2):
        pb, t = probs(scores[2 * pairs - 1 + sel], tops[sel])
        acc[sel] = kdot(kv_block(sel, here), pb, 0, 0)
        totals.append(t)

    def full_mix(j, total):
        pb, t = probs(scores[j], tops[1])
        acc[1] += kdot(kv_block(0, j), pb, 0, 0)
        return total + t

    totals[1] = lax.fori_loop(0, pairs, full_mix, totals[1])

    def off_mix(u, totals):
        low = u < here
        j = jnp.where(low, u, u + 1)
        sel = jnp.where(low, 0, 1)
        pb, t = probs(scores[pairs + u], jnp.where(low, tops[0], tops[1]))
        acc[sel] += kdot(kv_block(sel, j), pb, 0, 0)
        return (
            jnp.where(low, totals[0] + t, totals[0]),
            jnp.where(low, totals[1], totals[1] + t),
        )

    totals = lax.fori_loop(0, pairs - 1, off_mix, tuple(totals))
    for sel in range(2):
        total = jnp.sum(totals[sel], axis=0, keepdims=True)
        lse_ref[sel] = tops[sel] + jnp.log(total)
        mixed = acc[sel, HD:, :] / total
        for head in range(groups):
            att_ref[sel * blk : (sel + 1) * blk, head * HD : (head + 1) * HD] = (
                mixed[:, head * blk : (head + 1) * blk].T.astype(BF)
            )


def bwd_kernel(
    pairs, groups, blk, scale, idx_ref, q_ref, do_ref, att_ref, lse_ref, rope_ref, *refs
):
    kv_refs = refs[:pairs]
    gq_ref, gsum_ref = refs[pairs : pairs + 2]
    dkv_refs = refs[pairs + 2 : 2 * pairs + 2]
    kv_all, qp, dop, dkv, dq_acc = refs[2 * pairs + 2 :]
    here = idx_ref[0]
    core = idx_ref[1]
    for k in range(pairs):
        kv_all[k] = kv_refs[k][...]
    zeros = jnp.zeros((blk, HD), BF)
    for sel in range(2):
        for head in range(groups):
            rows = slice(head * blk, (head + 1) * blk)
            qp[sel, rows, :] = jnp.concatenate([head_rows(q_ref, sel, head, blk), zeros], axis=1)
            dop[sel, rows, :] = jnp.concatenate([zeros, head_rows(do_ref, sel, head, blk)], axis=1)
    prod = do_ref[...].astype(F32) * att_ref[...].astype(F32)
    picks_shape = (8, groups * HD)
    picks = (
        lax.broadcasted_iota(jnp.int32, picks_shape, 1) // HD
        == lax.broadcasted_iota(jnp.int32, picks_shape, 0)
    ).astype(F32)
    delta_heads = kdot(picks, prod, 1, 1, lax.Precision.HIGHEST)
    deltas = [
        jnp.concatenate(
            [delta_heads[h : h + 1, sel * blk : (sel + 1) * blk] for h in range(groups)], axis=1
        )
        for sel in range(2)
    ]
    lses = [lse_ref[0], lse_ref[1]]

    def kv_block(low_high, j):
        return kv_all[j ^ here, pl.ds(pl.multiple_of(low_high * blk, blk), blk), :]

    def terms(kv, sel, lse, delta, mask=None):
        s = kdot(kv, qp[sel], 1, 1)
        p = jnp.exp(s - lse) if mask is None else jnp.where(
            mask, jnp.exp(jnp.where(mask, s, -1e30) - lse), 0.0
        )
        dp = kdot(kv, dop[sel], 1, 1)
        ds = (p * (dp - delta)).astype(BF)
        pb = p.astype(BF)
        dk = kdot(ds, qp[sel], 1, 0) + kdot(pb, dop[sel], 1, 0)
        return ds, dk

    for sel in range(2):
        mask = diag_mask(blk, groups, (core == 1) if sel == 0 else (core == 0))
        kv = kv_block(sel, here)
        ds, dk = terms(kv, sel, lses[sel], deltas[sel], mask)
        dq_acc[sel] = kdot(kv, ds, 0, 0)
        dkv[here, sel] = dk

    def full_step(j, carry):
        kv = kv_block(0, j)
        ds, dk = terms(kv, 1, lses[1], deltas[1])
        dq_acc[1] += kdot(kv, ds, 0, 0)

        @pl.when(j == here)
        def _():
            dkv[j, 0] += dk

        @pl.when(j != here)
        def _():
            dkv[j, 0] = dk

        return carry

    lax.fori_loop(0, pairs, full_step, 0)

    def off_step(u, carry):
        low = u < here
        j = jnp.where(low, u, u + 1)
        sel = jnp.where(low, 0, 1)
        kv = kv_block(sel, j)
        ds, dk = terms(
            kv, sel, jnp.where(low, lses[0], lses[1]), jnp.where(low, deltas[0], deltas[1])
        )
        dq_acc[sel] += kdot(kv, ds, 0, 0)

        @pl.when(low)
        def _():
            dkv[j, 0] += dk
            dkv[j, 1] = jnp.zeros_like(dk)

        @pl.when(jnp.logical_not(low))
        def _():
            dkv[j, 1] = dk

        return carry

    lax.fori_loop(0, pairs - 1, off_step, 0)
    for k in range(pairs):
        for sel in range(2):
            dkv_refs[k][sel * blk : (sel + 1) * blk, :] = dkv[k ^ here, sel].astype(
                dkv_refs[k].dtype
            )
    for head in range(groups):
        cols = slice(head * HD, (head + 1) * HD)
        total = jnp.zeros((1, HD), F32)
        for sel in range(2):
            rows = slice(sel * blk, (sel + 1) * blk)
            cosine = rope_ref[0, :, rows]
            sine = rope_ref[1, :, rows]
            turned = dq_acc[sel, :HD, head * blk : (head + 1) * blk] * scale
            low, high = turned[: HD // 2], turned[HD // 2 :]
            back = jnp.concatenate(
                [low * cosine + high * sine, high * cosine - low * sine], axis=0
            ).T
            gq_ref[rows, cols] = back.astype(BF)
            total = total + jnp.sum(back, axis=0, keepdims=True)
        gsum_ref[:, cols] = total


VMEM_SPEC = pl.BlockSpec(memory_space=pltpu.VMEM)
SMEM_SPEC = pl.BlockSpec(memory_space=pltpu.SMEM)


def attention_fwd(idx, q, kvs):
    pairs = len(kvs)
    rows, cols = q.shape
    blk = rows // 2
    groups = cols // HD
    width = groups * blk
    return pl.pallas_call(
        functools.partial(fwd_kernel, pairs, groups, blk),
        out_shape=(
            jax.ShapeDtypeStruct((rows, cols), BF),
            jax.ShapeDtypeStruct((2, 1, width), F32),
        ),
        in_specs=[SMEM_SPEC] + [VMEM_SPEC] * (1 + pairs),
        out_specs=(VMEM_SPEC, VMEM_SPEC),
        scratch_shapes=[
            pltpu.VMEM((pairs, rows, 2 * HD), BF),
            pltpu.VMEM((2, width, 2 * HD), BF),
            pltpu.VMEM((2 * pairs + 1, blk, width), F32),
            pltpu.VMEM((2, 2 * HD, width), F32),
        ],
        compiler_params=pltpu.CompilerParams(vmem_limit_bytes=56 * 2**20),
        name="attn_fwd",
    )(idx, q, *kvs)


def attention_bwd(idx, q, d_out, att, lse, rope_t, kvs):
    pairs = len(kvs)
    rows, cols = q.shape
    blk = rows // 2
    groups = cols // HD
    width = groups * blk
    res = pl.pallas_call(
        functools.partial(bwd_kernel, pairs, groups, blk, 1.0 / math.sqrt(HD)),
        out_shape=(jax.ShapeDtypeStruct((rows, cols), BF), jax.ShapeDtypeStruct((1, cols), F32))
        + tuple(jax.ShapeDtypeStruct((rows, 2 * HD), BF) for _ in range(pairs)),
        in_specs=[SMEM_SPEC] + [VMEM_SPEC] * (5 + pairs),
        out_specs=(VMEM_SPEC,) * (2 + pairs),
        scratch_shapes=[
            pltpu.VMEM((pairs, rows, 2 * HD), BF),
            pltpu.VMEM((2, width, 2 * HD), BF),
            pltpu.VMEM((2, width, 2 * HD), BF),
            pltpu.VMEM((pairs, 2, blk, 2 * HD), F32),
            pltpu.VMEM((2, 2 * HD, width), F32),
        ],
        compiler_params=pltpu.CompilerParams(vmem_limit_bytes=56 * 2**20),
        name="attn_bwd",
    )(idx, q, d_out, att, lse, rope_t, *kvs)
    return res[0], res[1], res[2:]


def columns_kernel(groups_z, ff_blk, ff_wide, window, rows, idx_ref, gate_ref, up_ref, out_ref, win, sems):
    ff = gate_ref.shape[1]
    here = idx_ref[0]
    shifts = []
    copies = []
    for m, ref in enumerate((gate_ref, up_ref)):
        for g in range(groups_z):
            col = (g * 8 + here) * ff_blk
            start = jnp.minimum((col // 128) * 128, ff - window)
            if m == 0:
                shifts.append(col - start)
            copies.append(
                pltpu.make_async_copy(
                    ref.at[
                        pl.ds(pl.multiple_of(idx_ref[1] * rows, 16), rows),
                        pl.ds(pl.multiple_of(start, 128), window),
                    ],
                    win.at[m * groups_z + g],
                    sems.at[m * groups_z + g],
                )
            )
    for copy in copies:
        copy.start()
    pieces = [[None] * (ff_wide // 128) for _ in range(2)]
    for g in range(groups_z):
        first = g * ff_blk // 128
        lead = g * ff_blk - first * 128
        tiles = -(-(lead + ff_blk) // 128)
        row = lax.broadcasted_iota(jnp.int32, (window, tiles * 128), 0)
        lane = lax.broadcasted_iota(jnp.int32, (window, tiles * 128), 1) - lead
        hot = jnp.logical_and(row == lane + shifts[g], jnp.logical_and(lane >= 0, lane < ff_blk))
        hot = hot.astype(F32).astype(BF)
        for m in range(2):
            copies[m * groups_z + g].wait()
            part = kdot(win[m * groups_z + g], hot, 1, 0)
            for t in range(tiles):
                tile = part[:, t * 128 : (t + 1) * 128]
                old = pieces[m][first + t]
                pieces[m][first + t] = tile if old is None else old + tile
    for m in range(2):
        for t, tile in enumerate(pieces[m]):
            col = m * ff_wide + t * 128
            out_ref[:, col : col + 128] = (
                jnp.zeros((out_ref.shape[0], 128), BF) if tile is None else tile.astype(BF)
            )


def hidden_columns(idx, gate, up, groups_z, ff_blk, ff_wide, rows):
    ff = gate.shape[1]
    window = min(-(-(ff_blk + 127) // 128) * 128, ff)
    return pl.pallas_call(
        functools.partial(columns_kernel, groups_z, ff_blk, ff_wide, window, rows),
        out_shape=jax.ShapeDtypeStruct((rows, 2 * ff_wide), BF),
        in_specs=[SMEM_SPEC, pl.BlockSpec(memory_space=pl.ANY), pl.BlockSpec(memory_space=pl.ANY)],
        out_specs=VMEM_SPEC,
        scratch_shapes=[
            pltpu.VMEM((2 * groups_z, rows, window), BF),
            pltpu.SemaphoreType.DMA((2 * groups_z,)),
        ],
        name="hidden_columns",
    )(idx, gate, up)


def mlp_kernel(idx_ref, *refs):
    n2_refs, cot_refs = refs[:8], refs[8:16]
    gu_refs, down_refs = refs[16:19], refs[19:22]
    keep_ref, send_ref, g_ref, act_ref, n2_all, cot_all, down_w = refs[22:29]
    gu_w = refs[29]
    wt = idx_ref[0]
    odd = idx_ref[1]
    tok = n2_refs[0].shape[0]
    wide = gu_w.shape[1] // 2
    down_half = down_refs[0].shape[0]
    for k in range(8):
        n2_all[k * tok : (k + 1) * tok, :] = n2_refs[k][...]
        cot_all[k * tok : (k + 1) * tok, :] = cot_refs[k][...]
    for full, (own, first, second) in ((gu_w, gu_refs), (down_w, down_refs)):
        half, quarter = own.shape[0], first.shape[0]
        for w in range(2):

            @pl.when(wt == w)
            def _():
                full[w * half : (w + 1) * half, :] = own[...]

            other = (1 - w) * half
            for z in range(2):

                @pl.when(jnp.logical_and(wt == w, odd == z))
                def _():
                    at = other + z * quarter
                    full[at : at + quarter, :] = first[...]
                    at = other + (1 - z) * quarter
                    full[at : at + quarter, :] = second[...]

    pad = wide - 2 * down_half
    if pad:
        down_w[2 * down_half :, :] = jnp.zeros((pad, down_w.shape[1]), BF)

    def chunk(start, out_ref, out_start):
        rows = pl.ds(start, 4 * tok)
        n2 = n2_all[rows, :]
        gate = kdot(n2, gu_w[:, :wide], 1, 0)
        up = kdot(n2, gu_w[:, wide:], 1, 0)
        grad_act = kdot(cot_all[rows, :], down_w[...], 1, 1)
        sig = jax.nn.sigmoid(gate)
        gated = gate * sig
        act_ref[rows, :] = (gated * up).astype(BF)
        g_gate = (grad_act * up * sig * (1.0 + gate * (1.0 - sig))).astype(BF)
        g_up = (grad_act * gated).astype(BF)
        g_ref[rows, :wide] = g_gate
        g_ref[rows, wide:] = g_up
        grad = kdot(g_gate, gu_w[:, :wide], 1, 1) + kdot(g_up, gu_w[:, wide:], 1, 1)
        out_ref[pl.ds(out_start, 4 * tok), :] = grad.astype(out_ref.dtype)

    chunk(4 * tok, send_ref, 0)
    chunk(0, keep_ref, 0)


def mlp(idx, n2, cot, gu, down):
    tok, dim = n2[0].shape
    wide2 = gu[0].shape[1]
    wide = wide2 // 2
    sds = jax.ShapeDtypeStruct
    return pl.pallas_call(
        mlp_kernel,
        out_shape=(
            sds((4 * tok, dim), F32),
            sds((4 * tok, dim), BF),
            sds((8 * tok, wide2), BF),
            sds((8 * tok, wide), BF),
            sds((8 * tok, dim), BF),
            sds((8 * tok, dim), BF),
            sds((wide, dim), BF),
        ),
        in_specs=[SMEM_SPEC] + [VMEM_SPEC] * 22,
        out_specs=(VMEM_SPEC,) * 7,
        scratch_shapes=[pltpu.VMEM((dim, wide2), BF)],
        compiler_params=pltpu.CompilerParams(vmem_limit_bytes=56 * 2**20),
        name="mlp",
    )(idx, *n2, *cot, *gu, *down)


def outer_kernel(blocks, idx_ref, att_ref, gh_ref, n1_ref, gq_ref, mine_ref, send_ref):
    half = gq_ref.shape[1]
    rows = mine_ref.shape[1] // 2
    upper = idx_ref[1] == 1
    second = idx_ref[0] == 1
    gh = jnp.where(upper, gh_ref[:, half:].astype(F32), gh_ref[:, :half].astype(F32)).astype(BF)
    for part, (left, right) in enumerate(((att_ref[...], gh), (n1_ref[...], gq_ref[...]))):
        full = kdot(left, right, 0, 0)
        cols = slice(part * half, (part + 1) * half)
        for b in range(blocks):
            low = full[2 * b * rows : (2 * b + 1) * rows]
            high = full[(2 * b + 1) * rows : (2 * b + 2) * rows]
            at = slice(b % 2 * rows, (b % 2 + 1) * rows)
            mine_ref[b // 2, at, cols] = jnp.where(second, high, low).astype(BF)
            send_ref[b // 2, at, cols] = jnp.where(second, low, high).astype(BF)


def outer_terms(idx, att, gh, n1, gq, blocks):
    dim = att.shape[1]
    shape = jax.ShapeDtypeStruct((blocks // 2, dim // blocks, 2 * gq.shape[1]), BF)
    return pl.pallas_call(
        functools.partial(outer_kernel, blocks),
        out_shape=(shape, shape),
        in_specs=[SMEM_SPEC] + [VMEM_SPEC] * 4,
        out_specs=(VMEM_SPEC, VMEM_SPEC),
        name="outer_terms",
    )(idx, att, gh, n1, gq)


def kv_tail_kernel(count, core_rows, cos_ref, sin_ref, n1_ref, wq_ref, gn1_ref, *refs):
    kv_refs = refs[:count]
    keep_ref, send_ref, gw_ref, sum_ref = refs[count:]
    total = kv_refs[0][...].astype(F32)
    for ref in kv_refs[1:]:
        total = total + ref[...].astype(F32)
    lane = lax.broadcasted_iota(jnp.int32, total.shape, 1)
    turned = jnp.where(lane < HD, total * sin_ref[:, : 2 * HD], 0.0)
    ahead = pltpu.roll(turned, 2 * HD - HD // 2, 1)
    behind = pltpu.roll(turned, HD // 2, 1)
    turned = jnp.where(lane < HD // 2, ahead, jnp.where(lane < HD, -behind, 0.0))
    grad = jnp.where(lane < HD, total * cos_ref[:, : 2 * HD], total) + turned
    sum_ref[...] = jnp.sum(grad, axis=0, keepdims=True)
    grad = grad.astype(BF)
    cols = wq_ref.shape[1]
    part = gn1_ref[...] + kdot(grad, wq_ref[:, cols - 2 * HD :], 1, 1)
    for b in range(2):
        at = slice(b * core_rows, (b + 1) * core_rows)
        own = 2 * b * core_rows
        keep_ref[at, :] = part[own : own + core_rows]
        send_ref[at, :] = part[own + core_rows : own + 2 * core_rows]
    gw_ref[...] = kdot(n1_ref[...], grad, 0, 0).astype(BF)


def kv_tail(cosine, sine, n1, wq, gn1_q, kvs):
    rows, dim = n1.shape
    sds = jax.ShapeDtypeStruct
    return pl.pallas_call(
        functools.partial(kv_tail_kernel, len(kvs), rows // 4),
        out_shape=(
            sds((rows // 2, dim), F32),
            sds((rows // 2, dim), F32),
            sds((dim, 2 * HD), BF),
            sds((1, 2 * HD), F32),
        ),
        in_specs=[VMEM_SPEC] * (5 + len(kvs)),
        out_specs=(VMEM_SPEC,) * 4,
        name="kv_tail",
    )(cosine, sine, n1, wq, gn1_q, *kvs)


def assemble_kernel(groups_z, ff_blk, ff_wide, factor, idx_ref, *refs):
    part_refs = refs[:8]
    gate_ref, up_ref, parts = refs[8:]
    for k in range(8):
        parts[k] = part_refs[k][...].astype(F32) * factor
    for plane in range(8):
        part = parts[plane ^ idx_ref[0]]
        for ref, start in ((gate_ref, 0), (up_ref, ff_wide)):
            for g in range(groups_z):
                col = (g * 8 + plane) * ff_blk
                ref[:, col : col + ff_blk] = part[:, start + g * ff_blk : start + (g + 1) * ff_blk]


def assemble(idx, parts, groups_z, ff_blk, ff_wide, factor):
    rows = parts[0].shape[0]
    shape = jax.ShapeDtypeStruct((rows, 8 * groups_z * ff_blk), F32)
    return pl.pallas_call(
        functools.partial(assemble_kernel, groups_z, ff_blk, ff_wide, factor),
        out_shape=(shape, shape),
        in_specs=[SMEM_SPEC] + [VMEM_SPEC] * 8,
        out_specs=(VMEM_SPEC, VMEM_SPEC),
        scratch_shapes=[pltpu.VMEM((8, rows, 2 * ff_wide), F32)],
        name="assemble",
    )(idx, *parts)


def shards(block_input, cotangent, norm_attn, w_qkv, b_qkv, w_out, norm_mlp, w_gate, w_up, w_down):
    ctx_count = lax.axis_size(CTX)
    groups_z = ctx_count // 4
    pairs = ctx_count // 2
    device_count = 2 * ctx_count
    z_bits = groups_z.bit_length() - 1
    _, tok, dim = block_input.shape
    half_tok = tok // 2
    length = tok * ctx_count
    half_dim = dim // 2
    kv_cols = KVH * HD
    ff = w_gate.shape[1]
    ff_blk = ff // device_count
    factor = 1.0 / math.sqrt(2 * length)
    ctx = lax.axis_index(CTX)
    wt = lax.axis_index("wt")
    core = ctx % 2
    chip_y = (ctx // 2) % 2
    pair = ctx // 2
    group = ctx // 4
    plane = (ctx % 4) * 2 + wt

    def swap_of(a, cx, wx):
        if wx == 0:
            return lax.ppermute(a, CTX, [(i, i ^ cx) for i in range(ctx_count)])
        if cx == 0:
            return lax.ppermute(a, "wt", [(0, 1), (1, 0)])
        return lax.ppermute(
            a, CTX + ("wt",), [(i, i ^ (2 * cx + wx)) for i in range(device_count)]
        )

    def by_bit(bit, first, second, axis):
        return jnp.where(
            bit == 0,
            jnp.concatenate([first, second], axis=axis),
            jnp.concatenate([second, first], axis=axis),
        )

    def pick(a, index, axis=0):
        return lax.dynamic_index_in_dim(a, index, axis, keepdims=False)

    def pair_rows(own, peer):
        return jnp.concatenate(
            [own[:half_tok], peer[:half_tok], own[half_tok:], peer[half_tok:]], axis=0
        )

    def own_rows(a):
        return jnp.concatenate([a[:half_tok], a[tok : tok + half_tok]], axis=0)

    def peer_rows(a):
        return jnp.concatenate([a[half_tok:tok], a[tok + half_tok :]], axis=0)

    head_cols = dim // KVH
    rope_cols = head_cols + HD

    def core_cols(a, axis):
        pieces = [
            (head_cols * core, head_cols),
            (dim + HD * core, HD),
            (dim + kv_cols + HD * core, HD),
        ]
        return jnp.concatenate(
            [lax.dynamic_slice_in_dim(a, s, w, axis) for s, w in pieces], axis=axis
        )

    wq_own = core_cols(w_qkv, 1)
    wq_recv = swap_of(wq_own, 0, 1)
    x_own = block_input[0]
    x_two = pair_rows(x_own, swap_of(x_own, 1, 0)).astype(F32)
    b_own = core_cols(b_qkv, 0)

    ff_own = groups_z * ff_blk
    ff_pad = -ff_own % 128
    ff_wide = ff_own + ff_pad

    def plane_gather(a, filler=None):
        four = [a, swap_of(a, 0, 1), swap_of(a, 2, 0), swap_of(a, 2, 1)]
        if filler is not None:
            four = [a] + [after(v, filler) for v in four[1:]]
        return four + [swap_of(v, 1, 0) for v in four]

    def plane_quad(keep, send):
        quad = keep.astype(F32) + swap_of(send, 1, 0).astype(F32)
        return quad.reshape(4, tok, dim)

    def plane_sends(quad):
        return [
            swap_of(quad[1].astype(BF), 0, 1),
            swap_of(quad[2].astype(BF), 2, 0),
            swap_of(quad[3].astype(BF), 2, 1),
        ]

    def plane_finish(quad, recv):
        return quad[0] + recv[0].astype(F32) + recv[1].astype(F32) + recv[2].astype(F32)

    def ff_cols(p, part, gate, up, rows):
        at = jnp.stack([p, part]).astype(jnp.int32)
        return hidden_columns(at, gate, up, groups_z, ff_blk, ff_wide, rows)

    w_out_l, cot_own = after(w_out, wq_own), after(cotangent[0], wq_own)
    wo_recv = swap_of(lax.dynamic_slice_in_dim(w_out_l, half_dim * core, half_dim, 1), 0, 1)
    cot_all = plane_gather(cot_own)

    z_odd = group & 1
    gu_peer = ff_cols(plane ^ 1, z_odd, after(w_gate, wq_own), after(w_up, wq_own), half_dim // 2)

    def z_next_of(a):
        return lax.ppermute(a, CTX, [(i, i ^ 4) for i in range(ctx_count)])

    normed1, inv1 = rms_norm(x_two, norm_attn)
    normed1_bf = normed1.astype(BF)
    wq = by_bit(wt, wq_own, wq_recv, 0)
    project = dot(normed1_bf, wq) + b_own
    within = jnp.arange(half_tok, dtype=jnp.int32)
    peer = ctx ^ 1
    pos = jnp.concatenate(
        [
            ctx * half_tok + within,
            peer * half_tok + within,
            length - (ctx + 1) * half_tok + within,
            length - (peer + 1) * half_tok + within,
        ]
    )
    steps = jnp.arange(HD // 2, dtype=F32)
    angles = pos.astype(F32)[:, None] * (THETA ** (-2.0 * steps / HD))[None, :]
    cosine = jnp.tile(jnp.cos(angles), (1, 2 * rope_cols // HD))
    sine = jnp.tile(jnp.sin(angles), (1, 2 * rope_cols // HD))

    def halves(u):
        first = (lax.broadcasted_iota(jnp.int32, (1, u.shape[1]), 1) % HD) < HD // 2
        return first, jnp.roll(u, -(HD // 2), axis=1), jnp.roll(u, HD // 2, axis=1)

    def rope(u):
        first, ahead, behind = halves(u)
        return u * cosine + jnp.where(first, -ahead, behind) * sine

    rotated = rope(project[:, :rope_cols]).astype(BF)
    q_scaled = rotated[:, :head_cols] * BF(1.0 / math.sqrt(HD))
    kv_own = jnp.concatenate([rotated[:, head_cols:], project[:, rope_cols:].astype(BF)], axis=1)
    kvs = [kv_own] + [swap_of(kv_own, 2 * k, 0) for k in range(1, pairs)]

    w_down_l = after(w_down, kv_own)
    down_shape = (groups_z // 2, 8, ff_blk, dim)
    gu_first = swap_of(gu_peer, 0, 1)
    down_peer = w_down_l.reshape(2, -1, 8, ff_blk, dim)
    down_peer = pick(pick(down_peer, plane ^ 1, 2), z_odd).reshape(-1, dim)
    down_first = swap_of(down_peer, 0, 1)
    gu_second = z_next_of(after(gu_first, kv_own))
    down_second = z_next_of(after(down_first, kv_own))
    down_own = pick(w_down_l.reshape(down_shape), plane, 1).reshape(-1, dim)
    idx = jnp.stack([pair, core]).astype(jnp.int32)
    att_heads, lse = attention_fwd(idx, q_scaled, kvs)
    att_peer = swap_of(att_heads, 1, 0)
    wo_other = by_bit(core, wo_recv, swap_of(after(wo_recv, att_heads), 1, 0), 1)
    wo = by_bit(wt, w_out, wo_other, 0)
    att_peer = pair_rows(peer_rows(att_peer), own_rows(att_peer))
    att_two = by_bit(core, att_heads, att_peer, 1)
    hidden1 = x_own.astype(F32) + dot(own_rows(att_two), wo)
    normed2, inv2 = rms_norm(hidden1, norm_mlp)
    normed2_bf = normed2.astype(BF)
    w_gate_l, w_up_l = after(w_gate, normed2_bf), after(w_up, normed2_bf)
    gu_own = ff_cols(plane, jnp.int32(0), w_gate_l, w_up_l, half_dim)
    n2 = plane_gather(normed2_bf, (gu_own, down_own))

    keep, send, g_gu, active, n2_all, cot_all, down_w = mlp(
        jnp.stack([wt, z_odd]).astype(jnp.int32),
        n2,
        cot_all,
        (gu_own, gu_first, gu_second),
        (down_own, down_first, down_second),
    )
    gn2_quad = plane_quad(keep, send)
    out_keep = dot(active[: 4 * tok], down_w, 1, 0, BF)
    out_send = dot(active[4 * tok :], down_w, 1, 0, BF)
    n2_l, active_l = after(n2_all, gn2_quad), after(active, gn2_quad)
    gw_down = dot(active_l, cot_all, 0, 0, BF)
    gw_gu = dot(n2_l, g_gu, 0, 0, BF)

    def z_half_send(a, bit):
        a = a.reshape((a.shape[0] // 2, 2) + a.shape[1:])
        mine_bit = (group >> bit) & 1
        send = pick(a, 1 - mine_bit, 1)
        mask = 4 << bit
        recv = lax.ppermute(send, CTX, [(i, i ^ mask) for i in range(ctx_count)])
        return pick(a, mine_bit, 1), recv

    def z_half_add(pair_of):
        return pair_of[0].astype(F32) + pair_of[1].astype(F32)

    def z_half_more(pair_of, done):
        for bit in range(1, z_bits):
            part = z_half_add((pair_of[0], after(pair_of[1], done))).astype(BF)
            pair_of = z_half_send(part, bit)
        return pair_of, part

    def z_half_last(pair_of, done):
        return z_half_add((pair_of[0], gate(pair_of[1], done)))[0]

    gn_recv = plane_sends(gn2_quad)
    gn_recv[0] = after(gn_recv[0], (gw_gu, gw_down))
    grad_norm2 = plane_finish(gn2_quad, gn_recv)
    z_gu = z_half_send(gw_gu.reshape(groups_z, dim // groups_z, -1), 0)
    z_down = z_half_send(gw_down[:ff_own].reshape(groups_z, ff_blk, dim), 0)

    gg_mlp = jnp.sum(grad_norm2 * hidden1 * inv2, axis=0)
    grad_hidden = cot_own.astype(F32) + norm_back(grad_norm2, hidden1, inv2, norm_mlp)
    gh_own = grad_hidden.astype(BF)
    gh_two = pair_rows(gh_own, swap_of(gh_own, 1, 0))
    wo_rows = lax.dynamic_slice_in_dim(wo, half_dim * core, half_dim, 0)
    grad_att = dot(gh_two, wo_rows, 1, 1, BF)

    rope_t = jnp.stack([jnp.cos(angles).T, jnp.sin(angles).T])
    gq_bf, gq_sum, dkvs = attention_bwd(idx, q_scaled, grad_att, att_heads, lse, rope_t, kvs)
    dkv_recv = [dkvs[0]] + [swap_of(dkvs[k], 2 * k, 0) for k in range(1, pairs)]

    xc = jnp.stack([wt, core]).astype(jnp.int32)
    oq_mine, oq_send = outer_terms(xc, att_two, gh_two, normed1_bf, gq_bf, ctx_count)
    gn1_q = dot(gq_bf, wq[:, :head_cols], 1, 1)

    rows = dim // device_count

    def plane_step(a, bit, cx, wx):
        return pick(a, bit), swap_of(pick(a, 1 - bit), cx, wx)

    oq_recv = swap_of(oq_send, 0, 1)
    z_down, _ = z_half_more(z_down, gh_own)
    z_gu, _ = z_half_more(z_gu, oq_send)
    out_quad = plane_quad(out_keep, out_send)
    out_recv = plane_sends(out_quad)

    gn1_keep, gn1_send, gw_kv, gkv_sum = kv_tail(
        cosine, sine, normed1_bf, wq, gn1_q, dkv_recv
    )
    gn1_swap = swap_of(gn1_send, 1, 0)
    gb = jnp.concatenate([gq_sum[0], gkv_sum[0]])
    grad_norm1 = gn1_keep + gn1_swap
    x32 = x_own.astype(F32)
    inv1_own = own_rows(inv1)
    gg_attn = jnp.sum(grad_norm1 * x32 * inv1_own, axis=0)

    zero_q = jnp.zeros((head_cols,), F32)
    zero_h = jnp.zeros((HD,), F32)
    gb_full = jnp.concatenate(
        [
            by_bit(core, gb[:head_cols], zero_q, 0),
            by_bit(core, gb[head_cols:rope_cols], zero_h, 0),
            by_bit(core, gb[rope_cols:], zero_h, 0),
        ]
    )
    split_at = dim + kv_cols
    n_qk = split_at // device_count
    n_v = kv_cols // device_count
    small = jnp.concatenate(
        [
            gg_attn.reshape(device_count, rows),
            gg_mlp.reshape(device_count, rows),
            gb_full[:split_at].reshape(device_count, n_qk),
            gb_full[split_at:].reshape(device_count, n_v),
        ],
        axis=1,
    )
    n_small = small.shape[1]
    small = jnp.pad(small, ((0, 0), (0, 2 * HD - n_small)))
    tail = jnp.concatenate(
        [gw_kv.reshape(device_count, rows, 2 * HD), small.astype(BF)[:, None, :]], axis=1
    )
    tail_src = tail
    tail = tail.reshape(groups_z, 2, 2, 2, rows + 1, 2 * HD)
    tail = jnp.moveaxis(tail, (1, 3), (0, 1))
    kv_mine, kv_recv = plane_step(tail, chip_y, 2, 0)
    oq = (oq_mine.astype(F32) + gate(oq_recv, tail_src).astype(F32)).astype(BF)
    oq = jnp.moveaxis(oq.reshape(groups_z, 2, 2 * rows, 2 * head_cols), 1, 0)
    oq_mine, oq_recv = plane_step(oq, chip_y, 2, 0)
    tail = (kv_mine.astype(F32) + kv_recv.astype(F32)).astype(BF)
    kv_mine, kv_recv = plane_step(tail, wt, 0, 1)
    last = jnp.concatenate(
        [
            jnp.pad(
                (oq_mine.astype(F32) + gate(oq_recv, kv_mine).astype(F32)).reshape(
                    groups_z, 2, rows, 2 * head_cols
                ),
                ((0, 0), (0, 0), (0, 1), (0, 0)),
            ),
            kv_mine.astype(F32) + kv_recv.astype(F32),
        ],
        axis=-1,
    ).astype(BF)
    sum_gu = z_half_last(z_gu, last).astype(BF)
    sum_gu = sum_gu.reshape(8, rows, 2 * ff_wide)
    parts = [pick(sum_gu, plane)] + [
        swap_of(pick(sum_gu, plane ^ k), k >> 1, k & 1) for k in range(1, 8)
    ]
    last = last.reshape(ctx_count // 2, rows + 1, -1)
    last_all = lax.all_to_all(last, ("group", "core"), 0, 0, tiled=True)
    output = (hidden1 + plane_finish(out_quad, [gate(out_recv[0], last)] + out_recv[1:])).astype(BF)
    grad_input = grad_hidden + norm_back(after(grad_norm1, last), x32, inv1_own, norm_attn)
    shard_down = z_half_last(z_down, last) * factor
    last_all = last_all.reshape(groups_z, 2, rows + 1, -1).astype(F32)
    last_sum = jnp.sum(last_all, axis=0) * factor
    sum_oq, tail = last_sum[:, :rows, : 2 * head_cols], last_sum[:, :, 2 * head_cols :]
    shard_gate, shard_up = assemble(plane[None].astype(jnp.int32), parts, groups_z, ff_blk, ff_wide, factor)

    shard_wout = jnp.concatenate([sum_oq[0, :, :head_cols], sum_oq[1, :, :head_cols]], axis=1)
    low, high = tail[0], tail[1]
    shard_qkv = jnp.concatenate(
        [
            sum_oq[0, :, head_cols:],
            sum_oq[1, :, head_cols:],
            low[:rows, :HD],
            high[:rows, :HD],
            low[:rows, HD:],
            high[:rows, HD:],
        ],
        axis=1,
    )
    vec = low[rows, :n_small] + high[rows, :n_small]
    return (
        output[None],
        grad_input[None],
        vec[:rows],
        shard_qkv,
        vec[2 * rows : 2 * rows + n_qk],
        vec[2 * rows + n_qk :],
        shard_wout,
        vec[rows : 2 * rows],
        shard_gate,
        shard_up,
        shard_down,
    )


def solution(mesh):
    ctx_count, wt_count = mesh.devices.shape
    split = Mesh(mesh.devices.reshape(ctx_count // 4, 2, 2, wt_count), CTX + ("wt",))
    both = P(CTX + ("wt",))
    both_rows = P(CTX + ("wt",), None)
    tokens = P("wt", CTX, None)
    weight = P("wt", None)

    return jax.shard_map(
        shards,
        mesh=split,
        in_specs=(tokens, tokens, P(), weight, P(), weight, P(), weight, weight, weight),
        out_specs=(tokens, tokens, both, both_rows, both, both)
        + (both_rows, both, both_rows, both_rows, both_rows),
        check_vma=False,
    )
```
